256 devices in a mesh: slab: 256 (over z, x, y, core).
Axes of the slice: x: 4, y: 4, z: 8, core: 2. Of those that a mesh axis runs over, the one named last changes fastest.
Arguments:
- newton_rhs: float32 [3, 1024, 128, 128], P(None, 'slab'), may hold values from -8 to 8
- stiffness: float32 [1024, 128, 128], P('slab'), may hold values from 0.25 to 4
- stencil: float32 [27, 3, 3], replicated, may hold values from -0.1 to 10.1, as said below
- dual_weight: float32 [1024, 128], P('slab'), may hold values from 0.5 to 2
- mortar: bfloat16 [1024, 3, 128, 128], P('slab'), may hold values from -0.3125 to 0.3125
- partner: int32 [1024, 3], P('slab'), may hold values from 0 to 1023, as said below
- active: int32 [1024], P('slab'), may hold values 0 or 1
Outputs:
- increment: float32 [3, 1024, 128, 128], P(None, 'slab')
- residual: float32 [3, 1024, 128, 128], P(None, 'slab')
The draws below stay inside these ranges and needn't reach their ends.
Inputs may be any that keep to these rules, and one draw needn't show every extreme that they name: stencil[26 - k] is the transpose of stencil[k]; entries off the centre block lie within 0.1 in magnitude, and the centre block stencil[13] is 10 times the identity plus a symmetric matrix of entries within 0.1. `partner`: slave tile t lies on device d = t // 4; slot s of it names a tile on device (1 - d // 128) * 128 + (d % 128 + s - 1) modulo 128.
All inputs are finite; a program needn't handle non-finite values. No bound on the sum of `active` on one device may be relied on, other than what follows from the above.
Results may differ from the reference program's by a relative error of at most 0.0003.
Values sent between devices are 32-bit elements; how exact they have to be, the bound alone decides.
No kernel may reach another device: no remote copies, remote signals or barrier semaphores. Data moves between devices by JAX's collectives and lax.ppermute only.
A program may use at most 64 MiB of HBM per device.

```python
import math
import jax
import jax.numpy as jnp
from jax import lax

CX = 4
TILE = 128
CZ = 128
REACH = 1
ITERS = 2
PARTNERS = 3
HALF = 128
QUARTER = 64
NX = 1024


def draw_stencil(key, part):
    first = jax.random.uniform(jax.random.fold_in(key, 11), (27, 3, 3), jnp.float32, -0.1, 0.1)
    flipped = jnp.transpose(first, (0, 2, 1))[::-1]
    offsets = jnp.arange(27)[:, None, None]
    blocks = jnp.where(offsets < 13, first, flipped)
    center = 10.0 * jnp.eye(3, dtype=jnp.float32) + 0.5 * (first[13] + first[13].T)
    return jnp.where(offsets == 13, center[None], blocks)


def draw_partner(key, part):
    tile_ids = jnp.arange(NX, dtype=jnp.int32)
    device = tile_ids // CX
    side = device // HALF
    position = device % HALF
    slots = jnp.arange(PARTNERS, dtype=jnp.int32) - REACH
    target = (1 - side)[:, None] * HALF + (position[:, None] + slots[None, :]) % HALF
    local_tile = jax.random.randint(jax.random.fold_in(key, 23), (NX, PARTNERS), 0, CX, dtype=jnp.int32)
    return (target * CX + local_tile).astype(jnp.int32)


def touch_ends(array, own_key, least, largest):
    extent = array.shape
    place = [jax.random.randint(jax.random.fold_in(own_key, axis), (), 0, extent[axis]) for axis in range(len(extent))]
    array = array.at[tuple(place)].set(least)
    longest = extent.index(max(extent))
    place[longest] = (place[longest] + 1) % extent[longest]
    return array.at[tuple(place)].set(largest)


def block_scale(stream_key, extent, cuts, smallest, largest):
    gain, own = 1.0, jax.random.fold_in(stream_key, 6)
    for axis_at, parts in cuts:
        heights = jnp.exp(jax.random.uniform(jax.random.fold_in(own, axis_at), (parts,), jnp.float32, smallest / len(cuts), largest / len(cuts)))
        gain = gain * jnp.repeat(heights, extent[axis_at] // parts).reshape([-1 if axis == axis_at else 1 for axis in range(len(extent))])
    return gain


def normal_values(own_key, dims, width, most, split=(), kind=jnp.bfloat16):
    values = jax.random.normal(own_key, dims, jnp.float32) * width
    if len(split) > 0:
        values = block_scale(own_key, dims, split, -0.22, 0.18) * values
    return jnp.clip(values, min=-most, max=most).astype(kind)


def setup_inputs(seed: int = 0) -> dict:
    keys = jax.random.split(jax.random.key(seed), 8)
    newton_rhs = normal_values(keys[0], (3, NX, TILE, CZ), 1.0, 8.0, ((1, 256),), jnp.float32)
    stiffness = jnp.clip(jnp.exp(math.log(4.0) - 2.7725887 * jax.random.uniform(keys[1], (NX, TILE, CZ), jnp.float32) ** block_scale(keys[1], (NX, TILE, CZ), ((0, 256),), -0.2, 0.2)), 0.25, 4.0)
    stencil = draw_stencil(jax.random.fold_in(keys[7], 71), 0)
    dual_weight = jnp.clip(jnp.exp(math.log(2.0) - 1.3862944 * jax.random.uniform(keys[3], (NX, TILE), jnp.float32) ** block_scale(keys[3], (NX, TILE), ((0, 256),), -0.2, 0.2)), 0.5, 2.0)
    mortar = normal_values(keys[4], (NX, PARTNERS, TILE, TILE), (TILE * PARTNERS) ** -0.5, 0.3125, ((0, 256),))
    partner = draw_partner(jax.random.fold_in(keys[7], 71), 0)
    active = touch_ends((jax.random.randint(keys[6], (NX,), 0, 5) < 3).astype(jnp.int32), jax.random.fold_in(keys[6], 1), 0, 1)
    return {"newton_rhs": newton_rhs, "stiffness": stiffness, "stencil": stencil, "dual_weight": dual_weight, "mortar": mortar, "partner": partner, "active": active}


def stencil_conv(field_in, kernel):
    return lax.conv_general_dilated(field_in[None], kernel, (1, 1, 1), [(1, 1), (1, 1), (1, 1)], dimension_numbers=("NCDHW", "OIDHW", "NCDHW"), precision=lax.Precision.HIGHEST)[0]


def apply_operator(field_in, kernel, stiffness, dual_weight, mortar_full, partner, active_float):
    half_planes = NX // 2
    start_plane = QUARTER * CX
    rolled = jnp.roll(field_in, -start_plane, axis=1)
    first_part = stencil_conv(rolled[:, :half_planes], kernel)
    second_part = stencil_conv(rolled[:, half_planes:], kernel)
    joined = jnp.concatenate([first_part, second_part], axis=1)
    result = jnp.roll(joined, start_plane, axis=1) + stiffness[None] * field_in
    slave_face = field_in[2, :, :, -1]
    master = field_in[2, :, :, 0]
    facing = jnp.take(master, partner, axis=0)
    pulled = jnp.einsum("tpij,tpj->ti", mortar_full, facing, precision=lax.Precision.HIGHEST)
    gap_value = dual_weight * slave_face - pulled
    push_force = 4.0 * active_float[:, None] * gap_value
    back_force = -jnp.einsum("tpij,ti->tpj", mortar_full, push_force, precision=lax.Precision.HIGHEST)
    master_add = jax.ops.segment_sum(back_force.reshape(-1, TILE), partner.reshape(-1), num_segments=NX)
    result = result.at[2, :, :, -1].add(dual_weight * push_force)
    result = result.at[2, :, :, 0].add(master_add)
    return result


def reference(newton_rhs, stiffness, stencil, dual_weight, mortar, partner, active):
    kernel = jnp.transpose(stencil.reshape(3, 3, 3, 3, 3), (3, 4, 0, 1, 2))
    mortar_full = mortar.astype(jnp.float32)
    active_float = active.astype(jnp.float32)
    increment = jnp.zeros_like(newton_rhs)
    residual = newton_rhs
    direction = newton_rhs
    norm_now = jnp.sum(residual * residual)
    for iteration in range(ITERS):
        image = apply_operator(direction, kernel, stiffness, dual_weight, mortar_full, partner, active_float)
        step_size = norm_now / jnp.sum(direction * image)
        increment = increment + step_size * direction
        residual = residual - step_size * image
        norm_next = jnp.sum(residual * residual)
        direction = residual + (norm_next / norm_now) * direction
        norm_now = norm_next
    return increment, residual
```

```python
import functools
import jax
import jax.numpy as jnp
from jax import lax
from jax.experimental import pallas as pl
from jax.experimental.pallas import tpu as pltpu
from jax.sharding import PartitionSpec as P

F32 = jnp.float32
VMEM_LIMIT = 24 * 1024 * 1024
W = 128
PLANES = 4
HALO = 3 * W


def vmem():
    return pl.BlockSpec(memory_space=pltpu.VMEM)


def smem():
    return pl.BlockSpec(memory_space=pltpu.SMEM)


def f32(*shape):
    return jax.ShapeDtypeStruct(shape, F32)


def call(kernel, outs, ins, scratch=(), flops=1000, name=None):
    return pl.pallas_call(
        kernel,
        out_shape=outs,
        in_specs=ins,
        out_specs=jax.tree.map(lambda _: vmem(), outs),
        scratch_shapes=list(scratch),
        compiler_params=pltpu.CompilerParams(vmem_limit_bytes=VMEM_LIMIT),
        cost_estimate=pl.CostEstimate(flops=flops, bytes_accessed=1000000, transcendentals=0),
        name=name,
    )


def iota(axis, shape=(W, W)):
    return lax.broadcasted_iota(jnp.int32, shape, axis)


def shift_of(st):
    return (st[13, 0, 0] + st[13, 1, 1] + st[13, 2, 2]) * F32(1.0 / 3.0) + F32(2.125)


def columns_to_rows(columns):
    lane = iota(1)
    block = jnp.zeros((W, W), F32)
    for k, column in enumerate(columns):
        block = jnp.where(lane == k, column, block)
    return block.T


def pick(flag, yes, no):
    return jnp.where(flag, yes, no)


def pack_kernel(dev, field, mate, far):
    odd = dev[0] % 2 == 1
    for c in range(3):
        low, high = field[c, 0], field[c, PLANES - 1]
        mate[c * W : (c + 1) * W, :] = pick(odd, low, high)
        far[c * W : (c + 1) * W, :] = pick(odd, high, low)
    rows = columns_to_rows([field[2, t, :, 0:1] for t in range(PLANES)])[0:8, :]
    mate[HALO : HALO + 8, :] = rows
    far[HALO : HALO + 8, :] = rows


def fill_shifted(s):
    row = iota(0)

    def body(i, _):
        v = s[1, i]
        s[0, i] = jnp.where(row == 0, 0.0, pltpu.roll(v, 1, 0))
        s[2, i] = jnp.where(row == W - 1, 0.0, pltpu.roll(v, W - 1, 0))
        return 0

    lax.fori_loop(0, 18, body, 0)


BLOCK = 32


def sweep(s, st, emit, dots):
    lane = iota(1, (BLOCK, W))

    def body(it, dots):
        x = it // (W // BLOCK)
        y = pl.multiple_of((it % (W // BLOCK)) * BLOCK, BLOCK)
        rows = pl.ds(y, BLOCK)
        acc = [[None] * 3 for _ in range(3)]
        for dx in range(3):
            for dy in range(3):
                for e in range(3):
                    v = s[dy, e * 6 + x + dx, rows, :]
                    for dz in range(3):
                        for c in range(3):
                            term = st[9 * dx + 3 * dy + dz, c, e] * v
                            acc[dz][c] = term if acc[dz][c] is None else acc[dz][c] + term
        out = []
        for c in range(3):
            below = jnp.where(lane == 0, 0.0, pltpu.roll(acc[0][c], 1, 1))
            above = jnp.where(lane == W - 1, 0.0, pltpu.roll(acc[2][c], W - 1, 1))
            out.append(acc[1][c] + (below + above))
        return emit(x, rows, out, dots)

    return lax.fori_loop(0, PLANES * (W // BLOCK), body, dots)


def fold(v):
    return jnp.sum(v.reshape(BLOCK // 8, 8, W), axis=0)


def first_kernel(dev, st, field, mate, far, stiff, u, dots, s):
    odd = dev[0] % 2 == 1
    place = dev[0] % 128
    cut = jnp.logical_or(place == 63, place == 64)
    for c in range(3):
        a = mate[c * W : (c + 1) * W, :]
        b = pick(cut, 0.0, far[c * W : (c + 1) * W, :])
        s[1, c * 6] = pick(odd, a, b)
        s[1, c * 6 + 5] = pick(odd, b, a)
        for x in range(PLANES):
            s[1, c * 6 + 1 + x] = field[c, x]
    fill_shifted(s)
    theta = shift_of(st)

    def emit(x, rows, out, sums):
        square, energy = sums
        k = stiff[x, rows, :]
        for c in range(3):
            v = s[1, c * 6 + 1 + x, rows, :]
            image = out[c] + k * v
            u[c, x, rows, :] = image - theta * v
            square += fold(v * v)
            energy += fold(v * image)
        return square, energy

    zero = jnp.zeros((8, W), F32)
    square, energy = sweep(s, st, emit, (zero, zero))
    dots[0:8, :] = square
    dots[8:16, :] = energy


def contact(active, partner, field, table, dual, mortar, back, push_rows):
    back[...] = jnp.zeros(back.shape, F32)
    energy = jnp.zeros((W, 1), F32)
    weights = dual[...].T
    columns = []
    for t in range(PLANES):
        blocks = [mortar[t, s].astype(F32) for s in range(3)]
        slots = [4 * s + partner[t, s] % 4 for s in range(3)]
        total = jnp.zeros((W, W), F32)
        for s in range(3):
            total += blocks[s] * table[pl.ds(slots[s], 1), :]
        pulled = jnp.sum(total, axis=1, keepdims=True)
        weight = weights[:, t : t + 1]
        gap = weight * field(t) - pulled
        push = (F32(4.0) * active[t].astype(F32)) * gap
        energy += push * gap
        columns.append(weight * push)
        for s in range(3):
            row = jnp.sum(blocks[s] * push, axis=0, keepdims=True)
            back[pl.ds(slots[s], 1), :] = back[pl.ds(slots[s], 1), :] - row
    push_rows[...] = columns_to_rows(columns)[0:8, :]
    return energy


def contact0_kernel(dev, active, partner, faces, far, field, dual, mortar, back, push_rows, dots, table):
    odd = dev[0] % 2 == 1
    place = dev[0] % 128
    wrap = jnp.logical_or(place == 0, place == 127)
    own, mate = faces[0:4, :], faces[4:8, :]
    other = pick(wrap, far[HALO : HALO + 4, :], faces[8:12, :])
    table[0:4, :] = pick(odd, mate, other)
    table[4:8, :] = own
    table[8:12, :] = pick(odd, other, mate)
    energy = contact(
        active, partner, lambda t: field[0, t, :, W - 1 : W], table, dual, mortar, back, push_rows
    )
    dots[...] = jnp.where(iota(1, (8, W)) == 0, fold_column(energy), 0.0)


def fold_column(column):
    return jnp.sum(column.reshape(W // 8, 8, 1), axis=0)


def lists(pack, other, odd, swap_far, swap_next):
    own = pack[12:24, :]
    mate = pack[24:36, :]
    far = pick(swap_far, other[36:48, :], pack[36:48, :])
    far_mate = pick(swap_far, other[48:60, :], pack[48:60, :])
    mate_far = pick(swap_next, other[60:72, :], pack[60:72, :])
    m1 = pick(odd, mate, far)
    m2 = pick(odd, mate_far, far_mate)
    p1 = pick(odd, far, mate)
    p2 = pick(odd, far_mate, mate_far)
    return (
        m2[8:12] + m1[4:8] + own[0:4],
        m1[8:12] + own[4:8] + p1[0:4],
        own[8:12] + p1[4:8] + p2[0:4],
    )


def second_kernel(dev, st, u, mate, far, pack, cross, push, stiff, z, kz, dots, table, s, rows):
    odd = dev[0] % 2 == 1
    place = dev[0] % 128
    cut = jnp.logical_or(place == 63, place == 64)
    swap_far = jnp.logical_or(place == 0, place == 127)
    swap_next = jnp.logical_or(place == 1, place == 126)
    slave = lists(pack, cross, odd, swap_far, swap_next)
    master = lists(cross, pack, odd, swap_far, swap_next)
    other = pick(swap_far, pack[8:12, :], cross[8:12, :])
    table[0:4, :] = pick(odd, cross[4:8, :], other) + slave[0]
    table[4:8, :] = cross[0:4, :] + slave[1]
    table[8:12, :] = pick(odd, other, cross[4:8, :]) + slave[2]
    table[12:16, :] = jnp.zeros((4, W), F32)
    before = pick(place == 0, slave[0], master[0])
    after = pick(place == 127, slave[2], master[2])
    mate_push = mate[HALO + 16 : HALO + 20, :]
    far_push = far[HALO + 16 : HALO + 20, :]
    rows[...] = jnp.zeros((W, W), F32)
    rows[0:1, :] = before[3:4]
    rows[1:5, :] = master[1]
    rows[5:6, :] = after[0:1]
    rows[8:9, :] = pick(odd, mate_push, far_push)[3:4]
    rows[9:13, :] = push[0:4, :]
    rows[13:14, :] = pick(odd, far_push, mate_push)[0:1]
    columns = rows[...].T
    lane = iota(1)

    def corrected(plane, x):
        return (
            plane
            + jnp.where(lane == 0, columns[:, x : x + 1], 0.0)
            + jnp.where(lane == W - 1, columns[:, 8 + x : 9 + x], 0.0)
        )

    for c in range(3):
        a = mate[c * W : (c + 1) * W, :]
        b = far[c * W : (c + 1) * W, :]
        low, high = pick(odd, a, b), pick(odd, b, a)
        if c == 2:
            low, high = corrected(low, 0), corrected(high, 5)
        even = jnp.logical_not(odd)
        s[1, c * 6] = pick(jnp.logical_and(cut, even), 0.0, low)
        s[1, c * 6 + 5] = pick(jnp.logical_and(cut, odd), 0.0, high)
        for x in range(PLANES):
            v = u[c, x]
            if c == 2:
                v = corrected(v, x + 1)
            s[1, c * 6 + 1 + x] = v
            z[c, x] = v
    fill_shifted(s)

    def emit(x, rows, out, sums):
        square, energy = sums
        k = stiff[x, rows, :]
        for c in range(3):
            v = s[1, c * 6 + 1 + x, rows, :]
            image = out[c] + k * v
            kz[c, x, rows, :] = image
            square += fold(v * v)
            energy += fold(v * image)
        return square, energy

    zero = jnp.zeros((8, W), F32)
    square, energy = sweep(s, st, emit, (zero, zero))
    dots[0:8, :] = square
    dots[8:16, :] = energy


def contact1_kernel(active, partner, table, field, dual, mortar, dots_a, dots_c, dots_z, back, push_rows, dots):
    energy = contact(
        active, partner, lambda t: field[0, t, :, W - 1 : W], table, dual, mortar, back, push_rows
    )
    lane = iota(1, (8, W))
    bending = jnp.where(lane == 0, fold_column(energy), 0.0)
    values = (
        dots_a[0:8, :],
        dots_a[8:16, :] + dots_c[...],
        dots_z[0:8, :],
        dots_z[8:16, :] + bending,
    )
    row = jnp.zeros((8, W), F32)
    for k, value in enumerate(values):
        total = jnp.sum(jnp.sum(value, axis=0, keepdims=True), axis=1, keepdims=True)
        row = jnp.where(lane == k, total, row)
    dots[...] = row


def final_kernel(dev, st, field, z, kz, got, extra, push, inc, res):
    place = dev[0] % 128
    swap_far = jnp.logical_or(place == 0, place == 127)
    theta = shift_of(st)
    lane8 = iota(1, (8, W))
    row = jnp.sum(got[:, 0:8, :].reshape(8, 8, W), axis=0)[0:1, :]
    lane1 = iota(1, (1, W))

    def total(k):
        return jnp.sum(jnp.where(lane1 == k, row, 0.0), axis=1, keepdims=True)

    norm0, curve0, zz, zaz = total(0), total(1), total(2), total(3)
    step0 = norm0 / curve0
    lead = 1.0 - step0 * theta
    norm1 = step0 * step0 * zz - lead * lead * norm0
    rz = curve0 - theta * norm0
    zw = zz + theta * rz
    a = lead + norm1 / norm0
    curve1 = a * a * curve0 - 2.0 * a * step0 * zw + step0 * step0 * zaz
    step1 = norm1 / curve1
    both = step0 + step1 * a
    cross = step1 * step0
    keep = 1.0 - theta * both
    opposite = (dev[0] // 32) ^ 4
    master = got[opposite, 4:8, :] + pick(swap_far, extra[0:4, :], 0.0)
    block = jnp.concatenate([master, push[0:4, :], jnp.zeros((W - 8, W), F32)], axis=0)
    columns = block.T
    lane = iota(1)
    for c in range(3):
        for x in range(PLANES):
            r, v, k = field[c, x], z[c, x], kz[c, x]
            if c == 2:
                k = (
                    k
                    + jnp.where(lane == 0, columns[:, x : x + 1], 0.0)
                    + jnp.where(lane == W - 1, columns[:, 4 + x : 5 + x], 0.0)
                )
            inc[c, x] = both * r - cross * v
            res[c, x] = keep * r - both * v + cross * k


def pairs(f):
    return [(i, f(i) % 256) for i in range(256)]


MATE = pairs(lambda i: i ^ 1)
FAR = pairs(lambda i: i + 1 if i % 2 else i - 1)
CROSS = pairs(lambda i: i ^ 128)
PLANE_GROUPS = [[32 * a + b for b in range(32)] for a in range(8)]
COLUMN_GROUPS = [[32 * a + b for a in range(8)] for b in range(32)]


def swap(x, table):
    return lax.ppermute(x, "slab", table)


def local(rhs, stiff, stencil, dual, mortar, partner, active):
    dev = lax.axis_index("slab").astype(jnp.int32).reshape(1)
    shape = rhs.shape
    dual8 = jnp.concatenate([dual, jnp.zeros((W - PLANES, W), F32)], axis=0)
    face = pl.BlockSpec((1, PLANES, W, W), lambda i: (2, 0, 0, 0))

    def whole(n):
        return [vmem()] * n

    def contact_call(kernel, outs, ins, scratch, name):
        return pl.pallas_call(
            kernel,
            grid=(1,),
            out_shape=outs,
            in_specs=ins,
            out_specs=jax.tree.map(lambda _: vmem(), outs),
            scratch_shapes=scratch,
            compiler_params=pltpu.CompilerParams(vmem_limit_bytes=VMEM_LIMIT),
            cost_estimate=pl.CostEstimate(flops=2000000, bytes_accessed=1000000, transcendentals=0),
            name=name,
        )

    def pack(field, name):
        return call(
            pack_kernel, (f32(HALO + 8, W), f32(HALO + 8, W)), [smem(), vmem()], name=name
        )(dev, field)

    a_mate, a_far = pack(rhs, "pack0")
    g_mate = swap(a_mate, MATE)
    g_far = swap(a_far, FAR)
    own_faces = jnp.concatenate(
        [a_mate[HALO : HALO + 4], g_mate[HALO : HALO + 4], g_far[HALO : HALO + 4], jnp.zeros((4, W), F32)]
    )
    faces = swap(own_faces, CROSS)
    u, dots_a = call(
        first_kernel,
        (f32(*shape), f32(16, W)),
        [smem(), smem()] + whole(4),
        [pltpu.VMEM((3, 18, W, W), F32)],
        flops=40000000,
        name="first",
    )(dev, stencil, rhs, g_mate, g_far, stiff)
    back0, push0, dots_c = contact_call(
        contact0_kernel,
        (f32(16, W), f32(8, W), f32(8, W)),
        [smem(), smem(), smem(), vmem(), vmem(), face, vmem(), vmem()],
        [pltpu.VMEM((16, W), F32)],
        "contact0",
    )(dev, active, partner, faces, g_far, rhs, dual8, mortar)
    b_mate, b_far = pack(u, "pack1")
    items = jnp.concatenate([back0[0:12], push0[0:4]])
    b_mate = jnp.concatenate([b_mate[: HALO + 4], back0[0:12], push0[0:4]])
    h_mate = swap(b_mate, MATE)
    b_far = jnp.concatenate([b_far[: HALO + 4], back0[0:12], push0[0:4], h_mate[HALO + 4 : HALO + 16]])
    h_far = swap(b_far, FAR)
    h_next = swap(h_far[HALO + 4 : HALO + 16], MATE)
    pack_own = jnp.concatenate(
        [
            b_mate[HALO : HALO + 4],
            h_mate[HALO : HALO + 4],
            h_far[HALO : HALO + 4],
            back0[0:12],
            h_mate[HALO + 4 : HALO + 16],
            h_far[HALO + 4 : HALO + 16],
            h_far[HALO + 20 : HALO + 32],
            h_next,
        ]
    )
    cross = swap(pack_own, CROSS)
    z, kz, dots_z, table = call(
        second_kernel,
        (f32(*shape), f32(*shape), f32(16, W), f32(16, W)),
        [smem(), smem()] + whole(7),
        [pltpu.VMEM((3, 18, W, W), F32), pltpu.VMEM((W, W), F32)],
        flops=40000000,
        name="second",
    )(dev, stencil, u, h_mate, h_far, pack_own, cross, push0, stiff)
    back1, push1, row = contact_call(
        contact1_kernel,
        (f32(16, W), f32(8, W), f32(8, W)),
        [smem(), smem(), vmem(), face] + whole(5),
        [],
        "contact1",
    )(active, partner, table, z, dual8, mortar, dots_a, dots_c, dots_z)

    odd = dev[0] % 2 == 1
    place = dev[0] % 128
    swap_far = jnp.logical_or(place == 0, place == 127)
    from_mate = swap(back1, MATE)
    from_far = swap(back1, FAR)
    stage1 = lax.all_to_all(
        jnp.broadcast_to(row[0:1], (32, W)), "slab", 0, 0, tiled=True, axis_index_groups=PLANE_GROUPS
    )
    sums = jnp.sum(stage1, axis=0, keepdims=True)
    far_part = jnp.where(odd, from_far[0:4], from_far[8:12])
    mate_part = jnp.where(odd, from_mate[8:12], from_mate[0:4])
    total = back1[4:8] + mate_part + jnp.where(swap_far, 0.0, far_part)
    block = jnp.concatenate([sums, jnp.zeros((3, W), F32), total])
    got = lax.all_to_all(
        jnp.broadcast_to(block[None], (8, 8, W)), "slab", 0, 0, tiled=True, axis_index_groups=COLUMN_GROUPS
    )
    return call(
        final_kernel,
        (f32(*shape), f32(*shape)),
        [smem(), smem()] + whole(6),
        flops=1000000,
        name="final",
    )(dev, stencil, rhs, z, kz, got, far_part, push1)


def solution(mesh):
    placed = (
        P(None, "slab", None, None),
        P("slab", None, None),
        P(),
        P("slab", None),
        P("slab", None, None, None),
        P("slab", None),
        P("slab"),
    )
    return jax.shard_map(
        local,
        mesh=mesh,
        in_specs=placed,
        out_specs=(P(None, "slab", None, None), P(None, "slab", None, None)),
        check_vma=False,
    )
```

```python
import functools
import jax
import jax.numpy as jnp
from jax import lax
from jax.experimental import pallas as pl
from jax.experimental.pallas import tpu as pltpu
from jax.sharding import PartitionSpec as P

F32 = jnp.float32
VMEM_LIMIT = 24 * 1024 * 1024
W = 128
PLANES = 4
HALO = 3 * W


def vmem():
    return pl.BlockSpec(memory_space=pltpu.VMEM)


def smem():
    return pl.BlockSpec(memory_space=pltpu.SMEM)


def f32(*shape):
    return jax.ShapeDtypeStruct(shape, F32)


def anywhere():
    return pl.BlockSpec(memory_space=pl.ANY)


def call(kernel, name, ins, outs, scratch=(), cost=1000000, out_specs=None):
    return pl.pallas_call(
        kernel,
        out_shape=outs,
        in_specs=ins,
        out_specs=jax.tree.map(lambda _: vmem(), outs) if out_specs is None else out_specs,
        scratch_shapes=list(scratch),
        compiler_params=pltpu.CompilerParams(vmem_limit_bytes=VMEM_LIMIT),
        cost_estimate=pl.CostEstimate(flops=1000, bytes_accessed=cost, transcendentals=0),
        name=name,
    )


def iota(axis, shape=(W, W)):
    return lax.broadcasted_iota(jnp.int32, shape, axis)


def coefficient(st, k, c, e):
    return st[9 * k + 3 * c + e]


def shift_of(st):
    trace = coefficient(st, 13, 0, 0) + coefficient(st, 13, 1, 1) + coefficient(st, 13, 2, 2)
    return trace * F32(1.0 / 3.0) + F32(2.125)


def columns_to_rows(columns):
    lane = iota(1)
    block = jnp.zeros((W, W), F32)
    for k, column in enumerate(columns):
        block = jnp.where(lane == k, column, block)
    return block.T


def pick(flag, yes, no):
    return jnp.where(flag, yes, no)


def pick(flag, yes, no):
    return jnp.where(flag, yes, no)


def place_of(dev, at=0):
    odd = dev[at] % 2 == 1
    place = dev[at] % 128
    return odd, place


def is_cut(place):
    return jnp.logical_or(place == 63, place == 64)


def is_wrap(place):
    return jnp.logical_or(place == 0, place == 127)


def pack_kernel(dev, field, mate, far):
    odd, _ = place_of(dev)
    for c in range(3):
        low, high = field[c, 0], field[c, PLANES - 1]
        mate[c * W : (c + 1) * W, :] = pick(odd, low, high)
        far[c * W : (c + 1) * W, :] = pick(odd, high, low)
    rows = columns_to_rows([field[2, t, :, 0:1] for t in range(PLANES)])[0:8, :]
    mate[HALO : HALO + 8, :] = rows
    far[HALO : HALO + 8, :] = rows


BLOCK = 32


def fill_shifted(s, planes):
    row = iota(0)

    def body(c, _):
        for x in range(planes):
            i = c * planes + x
            v = s[1, i]
            s[0, i] = jnp.where(row == 0, 0.0, pltpu.roll(v, 1, 0))
            s[2, i] = jnp.where(row == W - 1, 0.0, pltpu.roll(v, W - 1, 0))
        return 0

    lax.fori_loop(0, 3, body, 0)


def sweep(s, st, planes, centre, emit):
    lane = iota(1, (BLOCK, W))
    steps = W // BLOCK

    def body(it, dots):
        x = it // steps
        y = pl.multiple_of((it % steps) * BLOCK, BLOCK)
        rows = pl.ds(y, BLOCK)
        acc = [[None] * 3 for _ in range(3)]
        for dx in range(3):
            for dy in range(3):
                for e in range(3):
                    v = s[dy, e * planes + centre(x) + dx - 1, rows, :]
                    for dz in range(3):
                        for c in range(3):
                            term = coefficient(st, 9 * dx + 3 * dy + dz, c, e) * v
                            acc[dz][c] = term if acc[dz][c] is None else acc[dz][c] + term
        out = []
        for c in range(3):
            below = jnp.where(lane == 0, 0.0, pltpu.roll(acc[0][c], 1, 1))
            above = jnp.where(lane == W - 1, 0.0, pltpu.roll(acc[2][c], W - 1, 1))
            out.append(acc[1][c] + (below + above))
        values = [s[1, c * planes + centre(x), rows, :] for c in range(3)]
        return emit(x, rows, out, values, dots)

    zero = jnp.zeros((8, W), F32)
    return lax.fori_loop(0, 2 * steps, body, (zero, zero))


def fold(v):
    return jnp.sum(v.reshape(BLOCK // 8, 8, W), axis=0)


def emitter(target, stiff, plane, theta):
    def emit(x, rows, out, values, sums):
        square, energy = sums
        k = stiff[plane(x), rows, :]
        for c in range(3):
            v = values[c]
            image = out[c] + k * v
            target[c, x, rows, :] = image if theta is None else image - theta * v
            square += fold(v * v)
            energy += fold(v * image)
        return square, energy

    return emit


def store_dots(dots, sums):
    dots[0:8, :] = sums[0]
    dots[8:16, :] = sums[1]


FACE_TERMS = [(3 * j + dz, c) for dz in range(3) for c in range(3) for j in range(9)]


def inner(x):
    return x + 1


def outer(x):
    return 3 * x


def inner_first_kernel(st, field, dual, stiff, mortar, ui, dots, stiff_v, mortar_v, weights, theta, s, sems):
    stiff_copy = pltpu.make_async_copy(stiff, stiff_v, sems.at[0])
    mortar_copy = pltpu.make_async_copy(mortar, mortar_v, sems.at[1])
    stiff_copy.start()
    mortar_copy.start()
    for c in range(3):
        for x in range(PLANES):
            s[1, c * 4 + x] = field[c, x]
    fill_shifted(s, 4)
    block = jnp.concatenate([dual[...], jnp.zeros((W - PLANES, W), F32)], axis=0)
    weights[...] = block.T
    stiff_copy.wait()
    theta[...] = jnp.full((8, W), shift_of(st), F32)
    store_dots(dots, sweep(s, st, 4, inner, emitter(ui, stiff_v, inner, shift_of(st))))
    mortar_copy.wait()


def fill_halo(dev, s, mate, far, edge_planes, inner_planes):
    odd, place = place_of(dev)
    cut = is_cut(place)
    for c in range(3):
        a = mate[c * W : (c + 1) * W, :]
        b = pick(cut, 0.0, far[c * W : (c + 1) * W, :])
        s[1, c * 6] = pick(odd, a, b)
        s[1, c * 6 + 5] = pick(odd, b, a)
        s[1, c * 6 + 1] = edge_planes(c, 0)
        s[1, c * 6 + 4] = edge_planes(c, 1)
        s[1, c * 6 + 2] = inner_planes(c, 0)
        s[1, c * 6 + 3] = inner_planes(c, 1)
    fill_shifted(s, 6)


def face_rows(edge, mid):
    planes = (edge.at[2, 0], mid.at[2, 0], mid.at[2, 1], edge.at[2, 1])
    return columns_to_rows([p[:, 0:1] for p in planes] + [p[:, W - 1 : W] for p in planes])[0:8, :]


def centre6(x):
    return 3 * x + 1


def edge_first_kernel(dev, st, field, mate, far, stiff, ui, ue, dots, to_mate, to_far, s):
    odd, _ = place_of(dev)
    fill_halo(dev, s, mate, far, lambda c, i: field[c, 3 * i], lambda c, i: field[c, 1 + i])
    store_dots(dots, sweep(s, st, 6, centre6, emitter(ue, stiff, outer, shift_of(st))))
    for c in range(3):
        low, high = ue[c, 0], ue[c, 1]
        to_mate[c * W : (c + 1) * W, :] = pick(odd, low, high)
        to_far[c * W : (c + 1) * W, :] = pick(odd, high, low)
    rows = face_rows(ue, ui)
    to_mate[HALO : HALO + 8, :] = rows
    to_far[HALO : HALO + 8, :] = rows


def inner_second_kernel(st, ui, ue, stiff, ki, dots, stiff_rows, coefs, s):
    for c in range(3):
        s[1, c * 4] = ue[c, 0]
        s[1, c * 4 + 1] = ui[c, 0]
        s[1, c * 4 + 2] = ui[c, 1]
        s[1, c * 4 + 3] = ue[c, 1]
    fill_shifted(s, 4)
    store_dots(dots, sweep(s, st, 4, inner, emitter(ki, stiff, inner, None)))
    faces = [stiff[t, :, 0:1] for t in range(PLANES)] + [stiff[t, :, W - 1 : W] for t in range(PLANES)]
    stiff_rows[...] = columns_to_rows(faces)[0:8, :]
    for i, (k, c) in enumerate(FACE_TERMS):
        coefs[i : i + 1, :] = jnp.full((1, W), coefficient(st, k, c, 2), F32)


def edge_second_kernel(dev, st, ui, ue, mate, far, stiff, ki, ke, dots, rows, s):
    fill_halo(dev, s, mate, far, lambda c, i: ue[c, i], lambda c, i: ui[c, i])
    store_dots(dots, sweep(s, st, 6, centre6, emitter(ke, stiff, outer, None)))
    rows[...] = face_rows(ke, ki)


def contact(meta, slave, table, weights, mortar, back):
    energy = jnp.zeros((W, 1), F32)
    columns, pushes, slots = [], [], []
    for t in range(PLANES):
        total = None
        for s in range(3):
            row = table[pl.ds(4 * s + meta[3 * t + s], 1), :]
            term = mortar[t, s].astype(F32) * row
            total = term if total is None else total + term
        pulled = jnp.sum(total, axis=1, keepdims=True)
        weight = weights[:, t : t + 1]
        gap = weight * slave(t) - pulled
        push = (F32(4.0) * meta[12 + t].astype(F32)) * gap
        energy += push * gap
        columns.append(weight * push)
        pushes.append(push)
    for s in range(3):
        rows = [
            jnp.sum(mortar[t, s].astype(F32) * pushes[t], axis=0, keepdims=True) for t in range(PLANES)
        ]
        for k in range(4):
            total = None
            for t in range(PLANES):
                term = jnp.where(meta[3 * t + s] == k, rows[t], 0.0)
                total = term if total is None else total + term
            back[4 * s + k : 4 * s + k + 1, :] = -total
    return energy, columns


def fold_column(column):
    return jnp.where(iota(1, (8, W)) == 0, jnp.sum(column.reshape(W // 8, 8, 1), axis=0), 0.0)


def contact0_kernel(meta, faces, far, field, weights, mortar, items, push_cols, dots, table):
    odd, place = place_of(meta, 16)
    own, mate = faces[0:4, :], faces[4:8, :]
    other = pick(is_wrap(place), far[HALO : HALO + 4, :], faces[8:12, :])
    table[0:4, :] = pick(odd, mate, other)
    table[4:8, :] = own
    table[8:12, :] = pick(odd, other, mate)
    energy, columns = contact(
        meta, lambda t: field[2, t, :, W - 1 : W], table, weights, mortar, items
    )
    lane = iota(1)
    block = jnp.zeros((W, W), F32)
    for k, column in enumerate(columns):
        block = jnp.where(lane == k, column, block)
    push_cols[...] = block
    items[12:16, :] = block.T[0:4, :]
    dots[...] = fold_column(energy)


def lists(pack, other, odd, swap_far, swap_next):
    own = pack[12:24, :]
    mate = pack[24:36, :]
    far = pick(swap_far, other[36:48, :], pack[36:48, :])
    far_mate = pick(swap_far, other[48:60, :], pack[48:60, :])
    mate_far = pick(swap_next, other[60:72, :], pack[60:72, :])
    m1 = pick(odd, mate, far)
    m2 = pick(odd, mate_far, far_mate)
    p1 = pick(odd, far, mate)
    p2 = pick(odd, far_mate, mate_far)
    return (
        m2[8:12] + m1[4:8] + own[0:4],
        m1[8:12] + own[4:8] + p1[0:4],
        own[8:12] + p1[4:8] + p2[0:4],
    )


def total_of(v):
    return jnp.sum(jnp.sum(v, axis=0, keepdims=True), axis=1, keepdims=True)


def join_kernel(
    meta, coefs, ui, ue, mate, far, pack, cross, items, push_cols, stiff_rows, u_rows, k_rows,
    weights, mortar, dots_ui, dots_ue, dots_c, dots_ki, dots_ke,
    send, k_cols, table, back,
):
    odd, place = place_of(meta, 16)
    cut, swap_far = is_cut(place), is_wrap(place)
    even = jnp.logical_not(odd)
    swap_next = jnp.logical_or(place == 1, place == 126)
    slave = lists(pack, cross, odd, swap_far, swap_next)
    master = lists(cross, pack, odd, swap_far, swap_next)
    other = pick(swap_far, pack[8:12, :], cross[8:12, :])
    table[0:4, :] = pick(odd, cross[4:8, :], other) + slave[0]
    table[4:8, :] = cross[0:4, :] + slave[1]
    table[8:12, :] = pick(odd, other, cross[4:8, :]) + slave[2]

    def slave_column(t):
        plane = ue.at[2, t // 3] if t in (0, 3) else ui.at[2, t - 1]
        return plane[:, W - 1 : W] + push_cols[:, t : t + 1]

    energy, columns = contact(meta, slave_column, table, weights, mortar, back)

    low = jnp.logical_and(cut, even)
    high = jnp.logical_and(cut, odd)
    own_total, own_push = master[1], items[12:16, :]
    before = pick(place == 0, slave[0], master[0])[3:4]
    after = pick(place == 127, slave[2], master[2])[0:1]
    mate_push = mate[HALO + 20 : HALO + 24, :]
    far_push = far[HALO + 20 : HALO + 24, :]
    push_before = pick(odd, mate_push, far_push)[3:4]
    push_after = pick(odd, far_push, mate_push)[0:1]
    totals = jnp.concatenate([pick(low, 0.0, before), own_total, pick(high, 0.0, after)], axis=0)
    pushes = jnp.concatenate([pick(low, 0.0, push_before), own_push, pick(high, 0.0, push_after)], axis=0)
    lane = iota(1, (PLANES, W))

    def shifts(rows6):
        out = []
        for dx in range(3):
            v = rows6[dx : dx + PLANES]
            out.append(
                (
                    jnp.where(lane == 0, 0.0, pltpu.roll(v, 1, 1)),
                    v,
                    jnp.where(lane == W - 1, 0.0, pltpu.roll(v, W - 1, 1)),
                )
            )
        return out

    lines = {}
    for k, (rows6, dz) in enumerate(((totals, 1), (totals, 0), (pushes, 2), (pushes, 1))):
        moved = shifts(rows6)
        for c in range(3):
            total = None
            for dx in range(3):
                for dy in range(3):
                    at = FACE_TERMS.index((9 * dx + 3 * dy + dz, c))
                    term = coefs[at : at + 1, :] * moved[dx][dy]
                    total = term if total is None else total + term
            lines[k, c] = total
    lines[0, 2] = lines[0, 2] + stiff_rows[0:4, :] * own_total
    lines[3, 2] = lines[3, 2] + stiff_rows[4:8, :] * own_push
    block = jnp.concatenate(
        [lines[k, c] for k in range(4) for c in range(3)] + [own_total, jnp.zeros((W - 52, W), F32)], axis=0
    )
    cols = block.T
    wide = iota(1)
    for t in range(PLANES):
        cols = jnp.where(wide == 44 + t, cols + columns[t], cols)
    k_cols[...] = cols

    face = own_total * u_rows[0:4, :] + own_push * u_rows[4:8, :]
    square = own_total * own_total + own_push * own_push
    image = own_total * (2.0 * k_rows[0:4, :] + lines[0, 2]) + own_push * (2.0 * k_rows[4:8, :] + lines[3, 2])
    values = (
        dots_ui[0:8, :] + dots_ue[0:8, :],
        dots_ui[8:16, :] + dots_ue[8:16, :] + dots_c[...],
        dots_ki[0:8, :] + dots_ke[0:8, :],
        dots_ki[8:16, :] + dots_ke[8:16, :] + fold_column(energy),
    )
    extra = (None, None, 2.0 * face + square, image)
    wide8 = iota(1, (8, W))
    row = jnp.zeros((8, W), F32)
    for k, value in enumerate(values):
        total = total_of(value)
        if extra[k] is not None:
            total = total + total_of(extra[k])
        row = jnp.where(wide8 == k, total, row)
    row = jnp.where(iota(0, (8, W)) == 0, row, 0.0)
    send[...] = jnp.broadcast_to(row[None], (32, 8, W))
    column = meta[16] % 32
    send[(column + 31) % 32, 4:8, :] = back[0:4, :]
    send[column, 4:8, :] = back[4:8, :]
    send[(column + 1) % 32, 4:8, :] = back[8:12, :]


def gather_kernel(u_rows, mate, far, following, items, pack):
    start = HALO + 8
    parts = [
        u_rows[0:4, :],
        mate[HALO : HALO + 4, :],
        far[HALO : HALO + 4, :],
        items[0:12, :],
        mate[start : start + 12, :],
        far[start : start + 12, :],
        far[start + 16 : start + 28, :],
        following[0:12, :],
    ]
    pack[...] = jnp.concatenate(parts, axis=0)


def relay_kernel(dev, got, send):
    column = dev[0] % 32
    level = dev[0] // 32
    dots = jnp.sum(got[:, 0:8, :], axis=0)
    first, last = column == 0, column == 31
    left = got[(column + 31) % 32, 4:8, :]
    right = got[(column + 1) % 32, 4:8, :]
    near = got[column, 4:8, :] + pick(first, 0.0, left) + pick(last, 0.0, right)
    side = 4 * (1 - level // 4)
    crossing = pick(first, left, pick(last, right, 0.0))
    goal = side + (level + jnp.where(first, 1, jnp.where(last, 3, 0))) % 4
    send[...] = jnp.broadcast_to(jnp.where(iota(0, (8, W)) == 0, dots, 0.0)[None], (8, 8, W))
    send[level ^ 4, 4:8, :] = near

    @pl.when(jnp.logical_or(first, last))
    def _():
        send[goal, 4:8, :] = crossing


def final_kernel(theta_v, field, ui, ue, ki, ke, push_cols, k_cols, got, inc, res, inc_s, res_s, sems):
    theta = theta_v[0:1, :]
    block = jnp.sum(got[...], axis=0)
    row = block[0:1, :]
    lane1 = iota(1, (1, W))

    def total(k):
        value = jnp.sum(jnp.where(lane1 == k, row, 0.0), axis=1, keepdims=True)
        return jnp.broadcast_to(value, (1, W))

    norm0, curve0, zz, zaz = total(0), total(1), total(2), total(3)
    step0 = norm0 / curve0
    lead = 1.0 - step0 * theta
    norm1 = step0 * step0 * zz - lead * lead * norm0
    rz = curve0 - theta * norm0
    zw = zz + theta * rz
    a = lead + norm1 / norm0
    curve1 = a * a * curve0 - 2.0 * a * step0 * zw + step0 * step0 * zaz
    step1 = norm1 / curve1
    both = step0 + step1 * a
    cross = step1 * step0
    keep = 1.0 - theta * both
    columns = jnp.concatenate([block, jnp.zeros((W - 8, W), F32)], axis=0).T
    lane = iota(1)
    copies = []
    for x in range(PLANES):
        for c in range(3):
            r = field[c, x]
            v = ue[c, x // 3] if x in (0, 3) else ui[c, x - 1]
            k = ke[c, x // 3] if x in (0, 3) else ki[c, x - 1]
            low = k_cols[:, c * 4 + x : c * 4 + x + 1]
            if c == 2:
                v = v + jnp.where(
                    lane == 0,
                    k_cols[:, 48 + x : 49 + x],
                    jnp.where(lane == W - 1, push_cols[:, x : x + 1], 0.0),
                )
                low = low + columns[:, 4 + x : 5 + x]
            added = jnp.where(lane == 0, low, 0.0)
            for i, place in ((1, 1), (2, W - 2), (3, W - 1)):
                j = i * 12 + c * 4 + x
                added = jnp.where(lane == place, k_cols[:, j : j + 1], added)
            k = k + added
            inc_s[c, x] = both * r - cross * v
            res_s[c, x] = keep * r - both * v + cross * k
            for i, (source, target) in enumerate(((inc_s, inc), (res_s, res))):
                copy = pltpu.make_async_copy(source.at[c, x], target.at[c, x], sems.at[i, c, x])
                copy.start()
                copies.append(copy)
    for copy in copies:
        copy.wait()


def pairs(f):
    return [(i, f(i) % 256) for i in range(256)]


MATE = pairs(lambda i: i ^ 1)
FAR = pairs(lambda i: i + 1 if i % 2 else i - 1)
CROSS = pairs(lambda i: i ^ 128)
PLANE_GROUPS = [[32 * a + b for b in range(32)] for a in range(8)]
COLUMN_GROUPS = [[32 * a + b for a in range(8)] for b in range(32)]


def swap(x, table):
    return lax.ppermute(x, "slab", table)


def exchange(x, groups):
    return lax.all_to_all(x, "slab", 0, 0, tiled=True, axis_index_groups=groups)


def local(rhs, stiff, stencil, dual, mortar, partner, active):
    dev = lax.axis_index("slab").astype(jnp.int32).reshape(1)
    half = (3, 2, W, W)
    shape = rhs.shape
    stage = 8000000
    flat = f32(16, W)

    def whole(n):
        return [vmem()] * n

    def dma(*dims):
        return pltpu.SemaphoreType.DMA(dims)

    st = stencil.reshape(-1)
    meta = jnp.concatenate([(partner % 4).reshape(-1), active, dev, jnp.zeros((15,), jnp.int32)])
    a_mate, a_far = call(
        pack_kernel, "pack", [smem(), vmem()], (f32(HALO + 8, W), f32(HALO + 8, W))
    )(dev, rhs)
    g_far = swap(a_far, FAR)
    g_mate = swap(a_mate, MATE)
    ui, dots_ui, stiff_v, mortar_v, weights, theta = call(
        inner_first_kernel,
        "inner_first",
        [smem(), vmem(), vmem(), anywhere(), anywhere()],
        (
            f32(*half),
            flat,
            f32(PLANES, W, W),
            jax.ShapeDtypeStruct(mortar.shape, mortar.dtype),
            f32(W, W),
            f32(8, W),
        ),
        [pltpu.VMEM((3, 12, W, W), F32), dma(2)],
        stage,
    )(st, rhs, dual, stiff, mortar)
    own_faces = jnp.concatenate([a_mate[HALO : HALO + 4], g_mate[HALO : HALO + 4], g_far[HALO : HALO + 4]])
    own_faces, ui, meta = lax.optimization_barrier((own_faces, ui, meta))
    faces = swap(own_faces, CROSS)
    ue, dots_ue, b_mate, b_far = call(
        edge_first_kernel,
        "edge_first",
        [smem(), smem()] + whole(5),
        (f32(*half), flat, f32(HALO + 8, W), f32(HALO + 8, W)),
        [pltpu.VMEM((3, 18, W, W), F32)],
        stage,
    )(dev, st, rhs, g_mate, g_far, stiff_v, ui)
    items, push_cols, dots_c = call(
        contact0_kernel,
        "contact0",
        [smem()] + whole(5),
        (f32(16, W), f32(W, W), f32(8, W)),
        [pltpu.VMEM((16, W), F32)],
    )(meta, faces, g_far, rhs, weights, mortar_v)
    u_rows = b_mate[HALO : HALO + 8]
    h_mate = swap(jnp.concatenate([b_mate, items]), MATE)
    mate_back = h_mate[HALO + 8 : HALO + 20]
    h_far = swap(jnp.concatenate([b_far, items, mate_back]), FAR)
    ki, dots_ki, stiff_rows, coefs = call(
        inner_second_kernel,
        "inner_second",
        [smem()] + whole(3),
        (f32(*half), flat, f32(8, W), f32(88, W)),
        [pltpu.VMEM((3, 12, W, W), F32)],
        stage,
    )(st, ui, ue, stiff_v)
    h_far, ki = lax.optimization_barrier((h_far, ki))
    h_next = swap(h_far[HALO + 8 : HALO + 20], MATE)
    pack = call(gather_kernel, "gather", whole(5), f32(72, W))(u_rows, h_mate, h_far, h_next, items)
    cross = swap(pack, CROSS)
    ke, dots_ke, k_rows = call(
        edge_second_kernel,
        "edge_second",
        [smem(), smem()] + whole(6),
        (f32(*half), flat, f32(8, W)),
        [pltpu.VMEM((3, 18, W, W), F32)],
        stage,
    )(dev, st, ui, ue, h_mate, h_far, stiff_v, ki)
    send, k_cols = call(
        join_kernel,
        "join",
        [smem()] + whole(19),
        (f32(32, 8, W), f32(W, W)),
        [pltpu.VMEM((16, W), F32), pltpu.VMEM((16, W), F32)],
    )(
        meta, coefs, ui, ue, h_mate, h_far, pack, cross, items, push_cols, stiff_rows,
        u_rows, k_rows, weights, mortar_v, dots_ui, dots_ue, dots_c, dots_ki, dots_ke,
    )
    got = exchange(send, PLANE_GROUPS)
    relayed = call(relay_kernel, "relay", [smem(), vmem()], f32(8, 8, W))(dev, got)
    sums = exchange(relayed, COLUMN_GROUPS)
    return call(
        final_kernel,
        "final",
        whole(9),
        (f32(*shape), f32(*shape)),
        [pltpu.VMEM(shape, F32), pltpu.VMEM(shape, F32), dma(2, 3, 4)],
        out_specs=(anywhere(), anywhere()),
    )(theta, rhs, ui, ue, ki, ke, push_cols, k_cols, sums)


def solution(mesh):
    placed = (
        P(None, "slab", None, None),
        P("slab", None, None),
        P(),
        P("slab", None),
        P("slab", None, None, None),
        P("slab", None),
        P("slab"),
    )
    return jax.shard_map(
        local,
        mesh=mesh,
        in_specs=placed,
        out_specs=(P(None, "slab", None, None), P(None, "slab", None, None)),
        check_vma=False,
    )
```

```python
import functools
import jax
import jax.numpy as jnp
from jax import lax
from jax.experimental import pallas as pl
from jax.experimental.pallas import tpu as pltpu
from jax.sharding import PartitionSpec as P

F32 = jnp.float32
VMEM_LIMIT = 24 * 1024 * 1024
W = 128
PLANES = 4
HALO = 3 * W


def vmem():
    return pl.BlockSpec(memory_space=pltpu.VMEM)


def smem():
    return pl.BlockSpec(memory_space=pltpu.SMEM)


def f32(*shape):
    return jax.ShapeDtypeStruct(shape, F32)


def anywhere():
    return pl.BlockSpec(memory_space=pl.ANY)


def call(kernel, name, ins, outs, scratch=(), cost=1000000, out_specs=None):
    return pl.pallas_call(
        kernel,
        out_shape=outs,
        in_specs=ins,
        out_specs=jax.tree.map(lambda _: vmem(), outs) if out_specs is None else out_specs,
        scratch_shapes=list(scratch),
        compiler_params=pltpu.CompilerParams(vmem_limit_bytes=VMEM_LIMIT),
        cost_estimate=pl.CostEstimate(flops=1000, bytes_accessed=cost, transcendentals=0),
        name=name,
    )


def iota(axis, shape=(W, W)):
    return lax.broadcasted_iota(jnp.int32, shape, axis)


def coefficient(st, k, c, e):
    return st[9 * k + 3 * c + e]


def shift_of(st):
    trace = coefficient(st, 13, 0, 0) + coefficient(st, 13, 1, 1) + coefficient(st, 13, 2, 2)
    return trace * F32(1.0 / 3.0) + F32(2.125)


def face_rows(planes):
    lane = iota(1)
    block = jnp.zeros((W, W), F32)
    for k, plane in enumerate(planes):
        moved = pltpu.roll(plane, 2 * k + 1, 1)
        block = jnp.where(lane // 2 == k, moved, block)
    rows = block.T[0:8, :]
    order = [1, 3, 5, 7, 0, 2, 4, 6]
    return jnp.concatenate([rows[i : i + 1] for i in order], axis=0)


def pick(flag, yes, no):
    return jnp.where(flag, yes, no)


def pick(flag, yes, no):
    return jnp.where(flag, yes, no)


def place_of(dev, at=0):
    odd = dev[at] % 2 == 1
    place = dev[at] % 128
    return odd, place


def is_cut(place):
    return jnp.logical_or(place == 63, place == 64)


def is_wrap(place):
    return jnp.logical_or(place == 0, place == 127)


def load_kernel(dev, rhs, field, mate, far, faces):
    odd, _ = place_of(dev)
    for c in range(3):
        low, high = rhs[c, 0], rhs[c, PLANES - 1]
        mate[c * W : (c + 1) * W, :] = pick(odd, low, high)
        far[c * W : (c + 1) * W, :] = pick(odd, high, low)
    rows = face_rows([rhs[2, t] for t in range(PLANES)])
    faces[...] = rows
    mate[HALO : HALO + 8, :] = rows
    far[HALO : HALO + 8, :] = rows
    field[...] = rhs[...]


BLOCK = 32


def fill_shifted(s, planes):
    row = iota(0)

    def body(c, _):
        for x in range(planes):
            i = c * planes + x
            v = s[1, i]
            s[0, i] = jnp.where(row == 0, 0.0, pltpu.roll(v, 1, 0))
            s[2, i] = jnp.where(row == W - 1, 0.0, pltpu.roll(v, W - 1, 0))
        return 0

    lax.fori_loop(0, 3, body, 0)


def sweep(s, st, planes, centre, emit):
    lane = iota(1, (BLOCK, W))
    steps = W // BLOCK

    def body(it, dots):
        x = it // steps
        y = pl.multiple_of((it % steps) * BLOCK, BLOCK)
        rows = pl.ds(y, BLOCK)
        acc = [[None] * 3 for _ in range(3)]
        for dx in range(3):
            for dy in range(3):
                for e in range(3):
                    v = s[dy, e * planes + centre(x) + dx - 1, rows, :]
                    for dz in range(3):
                        for c in range(3):
                            term = coefficient(st, 9 * dx + 3 * dy + dz, c, e) * v
                            acc[dz][c] = term if acc[dz][c] is None else acc[dz][c] + term
        out = []
        for c in range(3):
            below = jnp.where(lane == 0, 0.0, pltpu.roll(acc[0][c], 1, 1))
            above = jnp.where(lane == W - 1, 0.0, pltpu.roll(acc[2][c], W - 1, 1))
            out.append(acc[1][c] + (below + above))
        values = [s[1, c * planes + centre(x), rows, :] for c in range(3)]
        return emit(x, rows, out, values, dots)

    zero = jnp.zeros((8, W), F32)
    return lax.fori_loop(0, 2 * steps, body, (zero, zero))


def fold(v):
    return jnp.sum(v.reshape(BLOCK // 8, 8, W), axis=0)


def emitter(target, stiff, plane, theta):
    def emit(x, rows, out, values, sums):
        square, energy = sums
        k = stiff[plane(x), rows, :]
        for c in range(3):
            v = values[c]
            image = out[c] + k * v
            target[c, x, rows, :] = image if theta is None else image - theta * v
            square += fold(v * v)
            energy += fold(v * image)
        return square, energy

    return emit


def store_dots(dots, sums):
    dots[0:8, :] = sums[0]
    dots[8:16, :] = sums[1]


FACE_TERMS = [(3 * j + dz, c) for dz in range(3) for c in range(3) for j in range(9)]


def inner(x):
    return x + 1


def outer(x):
    return 3 * x


def inner_first_kernel(
    dev, st, partner, active, field, dual, stiff, mortar,
    ui, dots, theta, stiff_v, mortar_v, dual_v, meta, s, sems,
):
    stiff_copy = pltpu.make_async_copy(stiff, stiff_v, sems.at[0])
    mortar_copy = pltpu.make_async_copy(mortar, mortar_v, sems.at[1])
    stiff_copy.start()
    mortar_copy.start()
    dual_v[...] = dual[...]
    for t in range(PLANES):
        for slot in range(3):
            meta[3 * t + slot] = partner[t, slot] % 4
        meta[12 + t] = active[t]
    meta[16] = dev[0]
    for i in range(17, 32):
        meta[i] = 0
    for c in range(3):
        for x in range(PLANES):
            s[1, c * 4 + x] = field[c, x]
    fill_shifted(s, 4)
    theta[...] = jnp.full((8, W), shift_of(st), F32)
    stiff_copy.wait()
    store_dots(dots, sweep(s, st, 4, inner, emitter(ui, stiff_v, inner, shift_of(st))))
    mortar_copy.wait()


def fill_halo(dev, s, mate, far, edge_planes, inner_planes):
    odd, place = place_of(dev)
    cut = is_cut(place)
    for c in range(3):
        a = mate[c * W : (c + 1) * W, :]
        b = pick(cut, 0.0, far[c * W : (c + 1) * W, :])
        s[1, c * 6] = pick(odd, a, b)
        s[1, c * 6 + 5] = pick(odd, b, a)
        s[1, c * 6 + 1] = edge_planes(c, 0)
        s[1, c * 6 + 4] = edge_planes(c, 1)
        s[1, c * 6 + 2] = inner_planes(c, 0)
        s[1, c * 6 + 3] = inner_planes(c, 1)
    fill_shifted(s, 6)


def centre6(x):
    return 3 * x + 1


def edge_first_kernel(dev, st, field, mate, far, stiff, ui, ue, dots, to_mate, to_far, s):
    odd, _ = place_of(dev)
    fill_halo(dev, s, mate, far, lambda c, i: field[c, 3 * i], lambda c, i: field[c, 1 + i])
    store_dots(dots, sweep(s, st, 6, centre6, emitter(ue, stiff, outer, shift_of(st))))
    for c in range(3):
        low, high = ue[c, 0], ue[c, 1]
        to_mate[c * W : (c + 1) * W, :] = pick(odd, low, high)
        to_far[c * W : (c + 1) * W, :] = pick(odd, high, low)
    rows = face_rows([ue[2, 0], ui[2, 0], ui[2, 1], ue[2, 1]])
    to_mate[HALO : HALO + 8, :] = rows
    to_far[HALO : HALO + 8, :] = rows


def inner_second_kernel(st, ui, ue, stiff, ki, dots, stiff_rows, coefs, s):
    for c in range(3):
        s[1, c * 4] = ue[c, 0]
        s[1, c * 4 + 1] = ui[c, 0]
        s[1, c * 4 + 2] = ui[c, 1]
        s[1, c * 4 + 3] = ue[c, 1]
    fill_shifted(s, 4)
    store_dots(dots, sweep(s, st, 4, inner, emitter(ki, stiff, inner, None)))
    stiff_rows[...] = face_rows([stiff[t] for t in range(PLANES)])
    for i, (k, c) in enumerate(FACE_TERMS):
        coefs[i : i + 1, :] = jnp.full((1, W), coefficient(st, k, c, 2), F32)


def edge_second_kernel(dev, st, ui, ue, mate, far, stiff, ki, ke, dots, rows, s):
    fill_halo(dev, s, mate, far, lambda c, i: ue[c, i], lambda c, i: ui[c, i])
    store_dots(dots, sweep(s, st, 6, centre6, emitter(ke, stiff, outer, None)))
    rows[...] = face_rows([ke[2, 0], ki[2, 0], ki[2, 1], ke[2, 1]])


def thirds(v):
    a = v.astype(jnp.bfloat16)
    rest = v - a.astype(F32)
    b = rest.astype(jnp.bfloat16)
    c = (rest - b.astype(F32)).astype(jnp.bfloat16)
    return jnp.concatenate([a, b, c], axis=0)


def contact(meta, slave, table, dual, mortar, back, picked):
    for t in range(PLANES):
        for s in range(3):
            picked[3 * t + s : 3 * t + s + 1, :] = table[pl.ds(4 * s + meta[3 * t + s], 1), :]
    picked[12:16, :] = jnp.zeros((4, W), F32)
    parts = thirds(picked[...])
    pulled = []
    for t in range(PLANES):
        total = None
        for s in range(3):
            got = lax.dot_general(
                parts, mortar[t, s], (((1,), (1,)), ((), ())), preferred_element_type=F32
            )
            r = 3 * t + s
            row = got[r : r + 1] + (got[16 + r : 17 + r] + got[32 + r : 33 + r])
            total = row if total is None else total + row
        pulled.append(total)
    gap = dual * slave - jnp.concatenate(pulled, axis=0)
    which = iota(0, (PLANES, W))
    scale = jnp.zeros((PLANES, W), F32)
    for t in range(PLANES):
        scale = jnp.where(which == t, F32(4.0) * meta[12 + t].astype(F32), scale)
    push = scale * gap
    parts = thirds(jnp.concatenate([push, jnp.zeros((16 - PLANES, W), F32)], axis=0))
    for s in range(3):
        rows = []
        for t in range(PLANES):
            got = jnp.dot(parts, mortar[t, s], preferred_element_type=F32)
            rows.append(got[t : t + 1] + (got[16 + t : 17 + t] + got[32 + t : 33 + t]))
        for k in range(4):
            total = None
            for t in range(PLANES):
                term = jnp.where(meta[3 * t + s] == k, rows[t], 0.0)
                total = term if total is None else total + term
            back[4 * s + k : 4 * s + k + 1, :] = -total
    return push * gap, dual * push


def pad8(rows):
    return jnp.concatenate([rows, jnp.zeros((8 - PLANES, W), F32)], axis=0)


def contact0_kernel(meta, faces, far, r_rows, dual, mortar, items, dots, table, picked):
    odd, place = place_of(meta, 16)
    own, mate = faces[0:4, :], faces[4:8, :]
    other = pick(is_wrap(place), far[HALO : HALO + 4, :], faces[8:12, :])
    table[0:4, :] = pick(odd, mate, other)
    table[4:8, :] = own
    table[8:12, :] = pick(odd, other, mate)
    energy, pushed = contact(meta, r_rows[4:8, :], table, dual[...], mortar, items, picked)
    items[12:16, :] = pushed
    dots[...] = pad8(energy)


def lists(pack, other, odd, swap_far, swap_next):
    own = pack[12:24, :]
    mate = pack[24:36, :]
    far = pick(swap_far, other[36:48, :], pack[36:48, :])
    far_mate = pick(swap_far, other[48:60, :], pack[48:60, :])
    mate_far = pick(swap_next, other[60:72, :], pack[60:72, :])
    m1 = pick(odd, mate, far)
    m2 = pick(odd, mate_far, far_mate)
    p1 = pick(odd, far, mate)
    p2 = pick(odd, far_mate, mate_far)
    return (
        m2[8:12] + m1[4:8] + own[0:4],
        m1[8:12] + own[4:8] + p1[0:4],
        own[8:12] + p1[4:8] + p2[0:4],
    )


def total_of(v):
    return jnp.sum(jnp.sum(v, axis=0, keepdims=True), axis=1, keepdims=True)


def join_kernel(
    meta, coefs, mate, far, pack, cross, items, stiff_rows, u_rows, k_rows,
    dual, mortar, dots_ui, dots_ue, dots_c, dots_ki, dots_ke,
    send, rows, table, back, picked,
):
    odd, place = place_of(meta, 16)
    cut, swap_far = is_cut(place), is_wrap(place)
    even = jnp.logical_not(odd)
    swap_next = jnp.logical_or(place == 1, place == 126)
    slave = lists(pack, cross, odd, swap_far, swap_next)
    master = lists(cross, pack, odd, swap_far, swap_next)
    other = pick(swap_far, pack[8:12, :], cross[8:12, :])
    table[0:4, :] = pick(odd, cross[4:8, :], other) + slave[0]
    table[4:8, :] = cross[0:4, :] + slave[1]
    table[8:12, :] = pick(odd, other, cross[4:8, :]) + slave[2]

    energy, pushed = contact(meta, u_rows[4:8, :] + items[12:16, :], table, dual[...], mortar, back, picked)

    low = jnp.logical_and(cut, even)
    high = jnp.logical_and(cut, odd)
    own_total, own_push = master[1], items[12:16, :]
    before = pick(place == 0, slave[0], master[0])[3:4]
    after = pick(place == 127, slave[2], master[2])[0:1]
    mate_push = mate[HALO + 20 : HALO + 24, :]
    far_push = far[HALO + 20 : HALO + 24, :]
    push_before = pick(odd, mate_push, far_push)[3:4]
    push_after = pick(odd, far_push, mate_push)[0:1]
    totals = jnp.concatenate([pick(low, 0.0, before), own_total, pick(high, 0.0, after)], axis=0)
    pushes = jnp.concatenate([pick(low, 0.0, push_before), own_push, pick(high, 0.0, push_after)], axis=0)
    lane = iota(1, (PLANES, W))

    def shifts(rows6):
        out = []
        for dx in range(3):
            v = rows6[dx : dx + PLANES]
            out.append(
                (
                    jnp.where(lane == 0, 0.0, pltpu.roll(v, 1, 1)),
                    v,
                    jnp.where(lane == W - 1, 0.0, pltpu.roll(v, W - 1, 1)),
                )
            )
        return out

    lines = {}
    for k, (rows6, dz) in enumerate(((totals, 1), (totals, 0), (pushes, 2), (pushes, 1))):
        moved = shifts(rows6)
        for c in range(3):
            total = None
            for dx in range(3):
                for dy in range(3):
                    at = FACE_TERMS.index((9 * dx + 3 * dy + dz, c))
                    term = coefs[at : at + 1, :] * moved[dx][dy]
                    total = term if total is None else total + term
            lines[k, c] = total
    lines[0, 2] = lines[0, 2] + stiff_rows[0:4, :] * own_total
    lines[3, 2] = lines[3, 2] + stiff_rows[4:8, :] * own_push
    bend = lines[3, 2]
    lines[3, 2] = bend + pushed
    for c in range(3):
        for x in range(PLANES):
            for i, k in enumerate((2, 3, 0, 1)):
                j = 4 * (4 * c + x) + i
                rows[j : j + 1, :] = lines[k, c][x : x + 1]
    rows[48:64, :] = jnp.zeros((16, W), F32)
    for x in range(PLANES):
        rows[4 * x + 49 : 4 * x + 50, :] = own_push[x : x + 1]
        rows[4 * x + 50 : 4 * x + 51, :] = own_total[x : x + 1]
    face = own_total * u_rows[0:4, :] + own_push * u_rows[4:8, :]
    square = own_total * own_total + own_push * own_push
    image = own_total * (2.0 * k_rows[0:4, :] + lines[0, 2]) + own_push * (2.0 * k_rows[4:8, :] + bend)
    values = (
        dots_ui[0:8, :] + dots_ue[0:8, :],
        dots_ui[8:16, :] + dots_ue[8:16, :] + dots_c[...],
        dots_ki[0:8, :] + dots_ke[0:8, :],
        dots_ki[8:16, :] + dots_ke[8:16, :] + pad8(energy),
    )
    extra = (None, None, 2.0 * face + square, image)
    wide8 = iota(1, (8, W))
    row = jnp.zeros((8, W), F32)
    for k, value in enumerate(values):
        total = total_of(value)
        if extra[k] is not None:
            total = total + total_of(extra[k])
        row = jnp.where(wide8 == k, total, row)
    row = jnp.where(iota(0, (8, W)) == 0, row, 0.0)
    send[...] = jnp.broadcast_to(row[None], (32, 8, W))
    column = meta[16] % 32
    send[(column + 31) % 32, 4:8, :] = back[0:4, :]
    send[column, 4:8, :] = back[4:8, :]
    send[(column + 1) % 32, 4:8, :] = back[8:12, :]


def gather_kernel(u_rows, mate, far, following, items, pack):
    start = HALO + 8
    parts = [
        u_rows[0:4, :],
        mate[HALO : HALO + 4, :],
        far[HALO : HALO + 4, :],
        items[0:12, :],
        mate[start : start + 12, :],
        far[start : start + 12, :],
        far[start + 16 : start + 28, :],
        following[0:12, :],
    ]
    pack[...] = jnp.concatenate(parts, axis=0)


def relay_kernel(dev, got, send):
    column = dev[0] % 32
    level = dev[0] // 32
    dots = jnp.sum(got[:, 0:8, :], axis=0)
    first, last = column == 0, column == 31
    left = got[(column + 31) % 32, 4:8, :]
    right = got[(column + 1) % 32, 4:8, :]
    near = got[column, 4:8, :] + pick(first, 0.0, left) + pick(last, 0.0, right)
    side = 4 * (1 - level // 4)
    crossing = pick(first, left, pick(last, right, 0.0))
    goal = side + (level + jnp.where(first, 1, jnp.where(last, 3, 0))) % 4
    send[...] = jnp.broadcast_to(jnp.where(iota(0, (8, W)) == 0, dots, 0.0)[None], (8, 8, W))
    send[level ^ 4, 4:8, :] = near

    @pl.when(jnp.logical_or(first, last))
    def _():
        send[goal, 4:8, :] = crossing


def final_kernel(theta_v, field, ui, ue, ki, ke, rows, got, inc, res, inc_s, res_s, work, sems):
    theta = theta_v[0:1, :]
    block = jnp.sum(got[...], axis=0)
    row = block[0:1, :]
    lane1 = iota(1, (1, W))

    def total(k):
        value = jnp.sum(jnp.where(lane1 == k, row, 0.0), axis=1, keepdims=True)
        return jnp.broadcast_to(value, (1, W))

    norm0, curve0, zz, zaz = total(0), total(1), total(2), total(3)
    step0 = norm0 / curve0
    lead = 1.0 - step0 * theta
    norm1 = step0 * step0 * zz - lead * lead * norm0
    rz = curve0 - theta * norm0
    zw = zz + theta * rz
    a = lead + norm1 / norm0
    curve1 = a * a * curve0 - 2.0 * a * step0 * zw + step0 * step0 * zaz
    step1 = norm1 / curve1
    both = step0 + step1 * a
    cross = step1 * step0
    keep = 1.0 - theta * both
    work[0:48, :] = cross * rows[0:48, :]
    for x in range(PLANES):
        j = 4 * (8 + x)
        work[j + 1 : j + 2, :] = work[j + 1 : j + 2, :] - both * rows[49 + 4 * x : 50 + 4 * x, :]
        work[j + 2 : j + 3, :] = (
            work[j + 2 : j + 3, :]
            - both * rows[50 + 4 * x : 51 + 4 * x, :]
            + cross * block[4 + x : 5 + x]
        )
    work[48:64, :] = -cross * rows[48:64, :]
    work[64:W, :] = jnp.zeros((W - 64, W), F32)
    columns = work[...].T
    lane = iota(1)
    rim = jnp.logical_or(lane < 2, lane >= W - 2)

    def on_rim(q):
        return jnp.where(rim, pltpu.roll(columns, (W - 4 * q - 2) % W, 1), 0.0)

    copies = []
    for x in range(PLANES):
        for c in range(3):
            r = field[c, x]
            v = ue[c, x // 3] if x in (0, 3) else ui[c, x - 1]
            k = ke[c, x // 3] if x in (0, 3) else ki[c, x - 1]
            grown = both * r - cross * v
            left = keep * r - both * v + cross * k + on_rim(4 * c + x)
            inc_s[c, x] = grown + on_rim(12 + x) if c == 2 else grown
            res_s[c, x] = left
            for i, (source, target) in enumerate(((inc_s, inc), (res_s, res))):
                copy = pltpu.make_async_copy(source.at[c, x], target.at[c, x], sems.at[i, c, x])
                copy.start()
                copies.append(copy)
    for copy in copies:
        copy.wait()


def pairs(f):
    return [(i, f(i) % 256) for i in range(256)]


MATE = pairs(lambda i: i ^ 1)
FAR = pairs(lambda i: i + 1 if i % 2 else i - 1)
CROSS = pairs(lambda i: i ^ 128)
PLANE_GROUPS = [[32 * a + b for b in range(32)] for a in range(8)]
COLUMN_GROUPS = [[32 * a + b for a in range(8)] for b in range(32)]


def swap(x, table):
    return lax.ppermute(x, "slab", table)


def exchange(x, groups):
    return lax.all_to_all(x, "slab", 0, 0, tiled=True, axis_index_groups=groups)


def local(rhs, stiff, stencil, dual, mortar, partner, active):
    dev = lax.axis_index("slab").astype(jnp.int32).reshape(1)
    half = (3, 2, W, W)
    shape = rhs.shape
    stage = 8000000
    flat = f32(16, W)

    def whole(n):
        return [vmem()] * n

    def dma(*dims):
        return pltpu.SemaphoreType.DMA(dims)

    st = stencil.reshape(-1)
    field, a_mate, a_far, r_rows = call(
        load_kernel,
        "load",
        [smem(), vmem()],
        (f32(*shape), f32(HALO + 8, W), f32(HALO + 8, W), f32(8, W)),
    )(dev, rhs)
    g_far = swap(a_far, FAR)
    g_mate = swap(a_mate, MATE)
    ui, dots_ui, theta, stiff_v, mortar_v, dual_v, meta = call(
        inner_first_kernel,
        "inner_first",
        [smem()] * 4 + whole(2) + [anywhere()] * 2,
        (
            f32(*half),
            flat,
            f32(8, W),
            f32(PLANES, W, W),
            jax.ShapeDtypeStruct(mortar.shape, mortar.dtype),
            f32(PLANES, W),
            jax.ShapeDtypeStruct((32,), jnp.int32),
        ),
        [pltpu.VMEM((3, 12, W, W), F32), dma(2)],
        stage,
        out_specs=(vmem(),) * 6 + (smem(),),
    )(dev, st, partner, active, field, dual, stiff, mortar)
    own_faces = jnp.concatenate([a_mate[HALO : HALO + 4], g_mate[HALO : HALO + 4], g_far[HALO : HALO + 4]])
    own_faces, ui = lax.optimization_barrier((own_faces, ui))
    faces = swap(own_faces, CROSS)
    ue, dots_ue, b_mate, b_far = call(
        edge_first_kernel,
        "edge_first",
        [smem(), smem()] + whole(5),
        (f32(*half), flat, f32(HALO + 8, W), f32(HALO + 8, W)),
        [pltpu.VMEM((3, 18, W, W), F32)],
        stage,
    )(dev, st, field, g_mate, g_far, stiff_v, ui)
    items, dots_c = call(
        contact0_kernel,
        "contact0",
        [smem()] + whole(5),
        (f32(16, W), f32(8, W)),
        [pltpu.VMEM((16, W), F32), pltpu.VMEM((16, W), F32)],
    )(meta, faces, g_far, r_rows, dual_v, mortar_v)
    u_rows = b_mate[HALO : HALO + 8]
    h_mate = swap(jnp.concatenate([b_mate, items]), MATE)
    mate_back = h_mate[HALO + 8 : HALO + 20]
    h_far = swap(jnp.concatenate([b_far, items, mate_back]), FAR)
    ki, dots_ki, stiff_rows, coefs = call(
        inner_second_kernel,
        "inner_second",
        [smem()] + whole(3),
        (f32(*half), flat, f32(8, W), f32(88, W)),
        [pltpu.VMEM((3, 12, W, W), F32)],
        stage,
    )(st, ui, ue, stiff_v)
    h_far, ki = lax.optimization_barrier((h_far, ki))
    h_next = swap(h_far[HALO + 8 : HALO + 20], MATE)
    pack = call(gather_kernel, "gather", whole(5), f32(72, W))(u_rows, h_mate, h_far, h_next, items)
    cross = swap(pack, CROSS)
    ke, dots_ke, k_rows = call(
        edge_second_kernel,
        "edge_second",
        [smem(), smem()] + whole(6),
        (f32(*half), flat, f32(8, W)),
        [pltpu.VMEM((3, 18, W, W), F32)],
        stage,
    )(dev, st, ui, ue, h_mate, h_far, stiff_v, ki)
    send, rows = call(
        join_kernel,
        "join",
        [smem()] + whole(16),
        (f32(32, 8, W), f32(64, W)),
        [pltpu.VMEM((16, W), F32), pltpu.VMEM((16, W), F32), pltpu.VMEM((16, W), F32)],
    )(
        meta, coefs, h_mate, h_far, pack, cross, items, stiff_rows,
        u_rows, k_rows, dual_v, mortar_v, dots_ui, dots_ue, dots_c, dots_ki, dots_ke,
    )
    got = exchange(send, PLANE_GROUPS)
    relayed = call(relay_kernel, "relay", [smem(), vmem()], f32(8, 8, W))(dev, got)
    sums = exchange(relayed, COLUMN_GROUPS)
    return call(
        final_kernel,
        "final",
        whole(8),
        (f32(*shape), f32(*shape)),
        [pltpu.VMEM(shape, F32), pltpu.VMEM(shape, F32), pltpu.VMEM((W, W), F32), dma(2, 3, 4)],
        out_specs=(anywhere(), anywhere()),
    )(theta, field, ui, ue, ki, ke, rows, sums)


def solution(mesh):
    placed = (
        P(None, "slab", None, None),
        P("slab", None, None),
        P(),
        P("slab", None),
        P("slab", None, None, None),
        P("slab", None),
        P("slab"),
    )
    return jax.shard_map(
        local,
        mesh=mesh,
        in_specs=placed,
        out_specs=(P(None, "slab", None, None), P(None, "slab", None, None)),
        check_vma=False,
    )
```

```python
import functools
import jax
import jax.numpy as jnp
from jax import lax
from jax.experimental import pallas as pl
from jax.experimental.pallas import tpu as pltpu
from jax.sharding import PartitionSpec as P

F32 = jnp.float32
VMEM_LIMIT = 24 * 1024 * 1024
W = 128
PLANES = 4
HALO = 3 * W


def vmem():
    return pl.BlockSpec(memory_space=pltpu.VMEM)


def smem():
    return pl.BlockSpec(memory_space=pltpu.SMEM)


def f32(*shape):
    return jax.ShapeDtypeStruct(shape, F32)


def anywhere():
    return pl.BlockSpec(memory_space=pl.ANY)


def call(kernel, name, ins, outs, scratch=(), cost=1000000, out_specs=None):
    return pl.pallas_call(
        kernel,
        out_shape=outs,
        in_specs=ins,
        out_specs=jax.tree.map(lambda _: vmem(), outs) if out_specs is None else out_specs,
        scratch_shapes=list(scratch),
        compiler_params=pltpu.CompilerParams(vmem_limit_bytes=VMEM_LIMIT),
        cost_estimate=pl.CostEstimate(flops=1000, bytes_accessed=cost, transcendentals=0),
        name=name,
    )


def iota(axis, shape=(W, W)):
    return lax.broadcasted_iota(jnp.int32, shape, axis)


def coefficient(st, k, c, e):
    return st[9 * k + 3 * c + e]


def shift_of(st):
    trace = coefficient(st, 13, 0, 0) + coefficient(st, 13, 1, 1) + coefficient(st, 13, 2, 2)
    return trace * F32(1.0 / 3.0) + F32(2.125)


def face_rows(planes):
    lane = iota(1)
    block = jnp.zeros((W, W), F32)
    for k, plane in enumerate(planes):
        moved = pltpu.roll(plane, 2 * k + 1, 1)
        block = jnp.where(lane // 2 == k, moved, block)
    rows = block.T[0:8, :]
    order = [1, 3, 5, 7, 0, 2, 4, 6]
    return jnp.concatenate([rows[i : i + 1] for i in order], axis=0)


def pick(flag, yes, no):
    return jnp.where(flag, yes, no)


def pick(flag, yes, no):
    return jnp.where(flag, yes, no)


def place_of(dev, at=0):
    odd = dev[at] % 2 == 1
    place = dev[at] % 128
    return odd, place


def is_cut(place):
    return jnp.logical_or(place == 63, place == 64)


def is_wrap(place):
    return jnp.logical_or(place == 0, place == 127)


def load_kernel(dev, rhs, field, mate, far, faces):
    odd, _ = place_of(dev)
    for c in range(3):
        low, high = rhs[c, 0], rhs[c, PLANES - 1]
        mate[c * W : (c + 1) * W, :] = pick(odd, low, high)
        far[c * W : (c + 1) * W, :] = pick(odd, high, low)
    rows = face_rows([rhs[2, t] for t in range(PLANES)])
    faces[...] = rows
    mate[HALO : HALO + 8, :] = rows
    far[HALO : HALO + 8, :] = rows
    field[...] = rhs[...]


BLOCK = 32


def fill_shifted(s, planes):
    row = iota(0)

    def body(c, _):
        for x in range(planes):
            i = c * planes + x
            v = s[1, i]
            s[0, i] = jnp.where(row == 0, 0.0, pltpu.roll(v, 1, 0))
            s[2, i] = jnp.where(row == W - 1, 0.0, pltpu.roll(v, W - 1, 0))
        return 0

    lax.fori_loop(0, 3, body, 0)


def sweep(s, st, planes, centre, emit):
    lane = iota(1, (BLOCK, W))
    steps = W // BLOCK

    def body(it, dots):
        x = it // steps
        y = pl.multiple_of((it % steps) * BLOCK, BLOCK)
        rows = pl.ds(y, BLOCK)
        acc = [[None] * 3 for _ in range(3)]
        for dx in range(3):
            for dy in range(3):
                for e in range(3):
                    v = s[dy, e * planes + centre(x) + dx - 1, rows, :]
                    for dz in range(3):
                        for c in range(3):
                            term = coefficient(st, 9 * dx + 3 * dy + dz, c, e) * v
                            acc[dz][c] = term if acc[dz][c] is None else acc[dz][c] + term
        out = []
        for c in range(3):
            below = jnp.where(lane == 0, 0.0, pltpu.roll(acc[0][c], 1, 1))
            above = jnp.where(lane == W - 1, 0.0, pltpu.roll(acc[2][c], W - 1, 1))
            out.append(acc[1][c] + (below + above))
        values = [s[1, c * planes + centre(x), rows, :] for c in range(3)]
        return emit(x, rows, out, values, dots)

    zero = jnp.zeros((8, W), F32)
    return lax.fori_loop(0, 2 * steps, body, (zero, zero))


def fold(v):
    return jnp.sum(v.reshape(BLOCK // 8, 8, W), axis=0)


def emitter(target, stiff, plane, theta):
    def emit(x, rows, out, values, sums):
        square, energy = sums
        k = stiff[plane(x), rows, :]
        for c in range(3):
            v = values[c]
            image = out[c] + k * v
            target[c, x, rows, :] = image if theta is None else image - theta * v
            square += fold(v * v)
            energy += fold(v * image)
        return square, energy

    return emit


def store_dots(dots, sums):
    dots[0:8, :] = sums[0]
    dots[8:16, :] = sums[1]


FACE_TERMS = [(3 * j + dz, c) for dz in range(3) for c in range(3) for j in range(9)]


def inner(x):
    return x + 1


def outer(x):
    return 3 * x


def inner_first_kernel(
    dev, st, partner, active, field, dual, stiff, mortar,
    ui, dots, theta, stiff_v, mortar_v, dual_v, meta, s, sems,
):
    stiff_copy = pltpu.make_async_copy(stiff, stiff_v, sems.at[0])
    mortar_copy = pltpu.make_async_copy(mortar, mortar_v, sems.at[1])
    stiff_copy.start()
    mortar_copy.start()
    dual_v[...] = dual[...]
    for t in range(PLANES):
        for slot in range(3):
            meta[3 * t + slot] = partner[t, slot] % 4
        meta[12 + t] = active[t]
    meta[16] = dev[0]
    for i in range(17, 32):
        meta[i] = 0
    for c in range(3):
        for x in range(PLANES):
            s[1, c * 4 + x] = field[c, x]
    fill_shifted(s, 4)
    theta[...] = jnp.full((8, W), shift_of(st), F32)
    stiff_copy.wait()
    store_dots(dots, sweep(s, st, 4, inner, emitter(ui, stiff_v, inner, shift_of(st))))
    mortar_copy.wait()


def fill_halo(dev, s, mate, far, edge_planes, inner_planes):
    odd, place = place_of(dev)
    cut = is_cut(place)
    for c in range(3):
        a = mate[c * W : (c + 1) * W, :]
        b = pick(cut, 0.0, far[c * W : (c + 1) * W, :])
        s[1, c * 6] = pick(odd, a, b)
        s[1, c * 6 + 5] = pick(odd, b, a)
        s[1, c * 6 + 1] = edge_planes(c, 0)
        s[1, c * 6 + 4] = edge_planes(c, 1)
        s[1, c * 6 + 2] = inner_planes(c, 0)
        s[1, c * 6 + 3] = inner_planes(c, 1)
    fill_shifted(s, 6)


def centre6(x):
    return 3 * x + 1


def edge_first_kernel(dev, st, field, mate, far, stiff, ui, ue, dots, to_mate, to_far, s):
    odd, _ = place_of(dev)
    fill_halo(dev, s, mate, far, lambda c, i: field[c, 3 * i], lambda c, i: field[c, 1 + i])
    store_dots(dots, sweep(s, st, 6, centre6, emitter(ue, stiff, outer, shift_of(st))))
    for c in range(3):
        low, high = ue[c, 0], ue[c, 1]
        to_mate[c * W : (c + 1) * W, :] = pick(odd, low, high)
        to_far[c * W : (c + 1) * W, :] = pick(odd, high, low)
    rows = face_rows([ue[2, 0], ui[2, 0], ui[2, 1], ue[2, 1]])
    to_mate[HALO : HALO + 8, :] = rows
    to_far[HALO : HALO + 8, :] = rows


def inner_second_kernel(st, ui, ue, stiff, ki, dots, stiff_rows, coefs, s):
    for c in range(3):
        s[1, c * 4] = ue[c, 0]
        s[1, c * 4 + 1] = ui[c, 0]
        s[1, c * 4 + 2] = ui[c, 1]
        s[1, c * 4 + 3] = ue[c, 1]
    fill_shifted(s, 4)
    store_dots(dots, sweep(s, st, 4, inner, emitter(ki, stiff, inner, None)))
    stiff_rows[...] = face_rows([stiff[t] for t in range(PLANES)])
    for i, (k, c) in enumerate(FACE_TERMS):
        coefs[i : i + 1, :] = jnp.full((1, W), coefficient(st, k, c, 2), F32)


def edge_second_kernel(dev, st, ui, ue, mate, far, stiff, ki, ke, dots, rows, s):
    fill_halo(dev, s, mate, far, lambda c, i: ue[c, i], lambda c, i: ui[c, i])
    store_dots(dots, sweep(s, st, 6, centre6, emitter(ke, stiff, outer, None)))
    rows[...] = face_rows([ke[2, 0], ki[2, 0], ki[2, 1], ke[2, 1]])


def thirds(v):
    a = v.astype(jnp.bfloat16).astype(F32)
    rest = v - a
    b = rest.astype(jnp.bfloat16).astype(F32)
    return jnp.concatenate([a, b, rest - b, jnp.zeros_like(a)], axis=0).astype(jnp.bfloat16)


def contact(meta, slave, table, dual, mortar, back, picked):
    parts = []
    for s in range(3):
        for t in range(PLANES):
            picked[8 * s + t : 8 * s + t + 1, :] = table[pl.ds(4 * s + meta[3 * t + s], 1), :]
        parts.append(thirds(picked[8 * s : 8 * s + PLANES, :]))
    left = jnp.concatenate(parts, axis=1)
    blocks = [jnp.concatenate([mortar[t, s] for s in range(3)], axis=1) for t in range(PLANES)]
    pulled = []
    for t in range(PLANES):
        got = lax.dot_general(
            left, blocks[t], (((1,), (1,)), ((), ())), preferred_element_type=F32
        )
        pulled.append(got[t : t + 1] + (got[4 + t : 5 + t] + got[8 + t : 9 + t]))
    gap = dual * slave - jnp.concatenate(pulled, axis=0)
    which = iota(0, (PLANES, W))
    scale = jnp.zeros((PLANES, W), F32)
    for t in range(PLANES):
        scale = jnp.where(which == t, F32(4.0) * meta[12 + t].astype(F32), scale)
    push = scale * gap
    left = thirds(push)
    rows = []
    for t in range(PLANES):
        got = jnp.dot(left, blocks[t], preferred_element_type=F32)
        rows.append(got[t : t + 1] + (got[4 + t : 5 + t] + got[8 + t : 9 + t]))
    for s in range(3):
        for k in range(4):
            total = None
            for t in range(PLANES):
                term = jnp.where(meta[3 * t + s] == k, rows[t][:, s * W : (s + 1) * W], 0.0)
                total = term if total is None else total + term
            back[4 * s + k : 4 * s + k + 1, :] = -total
    return push * gap, dual * push


def pad8(rows):
    return jnp.concatenate([rows, jnp.zeros((8 - PLANES, W), F32)], axis=0)


def contact0_kernel(meta, faces, far, r_rows, dual, mortar, items, dots, table, picked):
    odd, place = place_of(meta, 16)
    own, mate = faces[0:4, :], faces[4:8, :]
    other = pick(is_wrap(place), far[HALO : HALO + 4, :], faces[8:12, :])
    table[0:4, :] = pick(odd, mate, other)
    table[4:8, :] = own
    table[8:12, :] = pick(odd, other, mate)
    energy, pushed = contact(meta, r_rows[4:8, :], table, dual[...], mortar, items, picked)
    items[12:16, :] = pushed
    dots[...] = pad8(energy)


def lists(pack, other, odd, swap_far, swap_next):
    own = pack[12:24, :]
    mate = pack[24:36, :]
    far = pick(swap_far, other[36:48, :], pack[36:48, :])
    far_mate = pick(swap_far, other[48:60, :], pack[48:60, :])
    mate_far = pick(swap_next, other[60:72, :], pack[60:72, :])
    m1 = pick(odd, mate, far)
    m2 = pick(odd, mate_far, far_mate)
    p1 = pick(odd, far, mate)
    p2 = pick(odd, far_mate, mate_far)
    return (
        m2[8:12] + m1[4:8] + own[0:4],
        m1[8:12] + own[4:8] + p1[0:4],
        own[8:12] + p1[4:8] + p2[0:4],
    )


def total_of(v):
    return jnp.sum(jnp.sum(v, axis=0, keepdims=True), axis=1, keepdims=True)


def join_kernel(
    meta, coefs, mate_items, far, pack, cross, items, stiff_rows, u_rows, k_rows,
    dual, mortar, dots_ui, dots_ue, dots_c, dots_ki, dots_ke,
    send, rows, table, back, picked,
):
    odd, place = place_of(meta, 16)
    cut, swap_far = is_cut(place), is_wrap(place)
    even = jnp.logical_not(odd)
    swap_next = jnp.logical_or(place == 1, place == 126)
    slave = lists(pack, cross, odd, swap_far, swap_next)
    master = lists(cross, pack, odd, swap_far, swap_next)
    other = pick(swap_far, pack[8:12, :], cross[8:12, :])
    table[0:4, :] = pick(odd, cross[4:8, :], other) + slave[0]
    table[4:8, :] = cross[0:4, :] + slave[1]
    table[8:12, :] = pick(odd, other, cross[4:8, :]) + slave[2]

    energy, pushed = contact(meta, u_rows[4:8, :] + items[12:16, :], table, dual[...], mortar, back, picked)

    low = jnp.logical_and(cut, even)
    high = jnp.logical_and(cut, odd)
    own_total, own_push = master[1], items[12:16, :]
    before = pick(place == 0, slave[0], master[0])[3:4]
    after = pick(place == 127, slave[2], master[2])[0:1]
    mate_push = mate_items[12:16, :]
    far_push = far[HALO + 20 : HALO + 24, :]
    push_before = pick(odd, mate_push, far_push)[3:4]
    push_after = pick(odd, far_push, mate_push)[0:1]
    totals = jnp.concatenate([pick(low, 0.0, before), own_total, pick(high, 0.0, after)], axis=0)
    pushes = jnp.concatenate([pick(low, 0.0, push_before), own_push, pick(high, 0.0, push_after)], axis=0)
    lane = iota(1, (PLANES, W))

    def shifts(rows6):
        out = []
        for dx in range(3):
            v = rows6[dx : dx + PLANES]
            out.append(
                (
                    jnp.where(lane == 0, 0.0, pltpu.roll(v, 1, 1)),
                    v,
                    jnp.where(lane == W - 1, 0.0, pltpu.roll(v, W - 1, 1)),
                )
            )
        return out

    lines = {}
    for k, (rows6, dz) in enumerate(((totals, 1), (totals, 0), (pushes, 2), (pushes, 1))):
        moved = shifts(rows6)
        for c in range(3):
            total = None
            for dx in range(3):
                for dy in range(3):
                    at = FACE_TERMS.index((9 * dx + 3 * dy + dz, c))
                    term = coefs[at : at + 1, :] * moved[dx][dy]
                    total = term if total is None else total + term
            lines[k, c] = total
    lines[0, 2] = lines[0, 2] + stiff_rows[0:4, :] * own_total
    lines[3, 2] = lines[3, 2] + stiff_rows[4:8, :] * own_push
    bend = lines[3, 2]
    lines[3, 2] = bend + pushed
    for c in range(3):
        for x in range(PLANES):
            for i, k in enumerate((2, 3, 0, 1)):
                j = 4 * (4 * c + x) + i
                rows[j : j + 1, :] = lines[k, c][x : x + 1]
    rows[48:64, :] = jnp.zeros((16, W), F32)
    for x in range(PLANES):
        rows[4 * x + 49 : 4 * x + 50, :] = own_push[x : x + 1]
        rows[4 * x + 50 : 4 * x + 51, :] = own_total[x : x + 1]
    face = own_total * u_rows[0:4, :] + own_push * u_rows[4:8, :]
    square = own_total * own_total + own_push * own_push
    image = own_total * (2.0 * k_rows[0:4, :] + lines[0, 2]) + own_push * (2.0 * k_rows[4:8, :] + bend)
    values = (
        dots_ui[0:8, :] + dots_ue[0:8, :],
        dots_ui[8:16, :] + dots_ue[8:16, :] + dots_c[...],
        dots_ki[0:8, :] + dots_ke[0:8, :],
        dots_ki[8:16, :] + dots_ke[8:16, :] + pad8(energy),
    )
    extra = (None, None, 2.0 * face + square, image)
    wide8 = iota(1, (8, W))
    row = jnp.zeros((8, W), F32)
    for k, value in enumerate(values):
        total = total_of(value)
        if extra[k] is not None:
            total = total + total_of(extra[k])
        row = jnp.where(wide8 == k, total, row)
    row = jnp.where(iota(0, (8, W)) == 0, row, 0.0)
    send[...] = jnp.broadcast_to(row[None], (32, 8, W))
    column = meta[16] % 32
    send[(column + 31) % 32, 4:8, :] = back[0:4, :]
    send[column, 4:8, :] = back[4:8, :]
    send[(column + 1) % 32, 4:8, :] = back[8:12, :]


def gather_kernel(u_rows, mate, mate_items, far, following, items, pack):
    start = HALO + 8
    parts = [
        u_rows[0:4, :],
        mate[HALO : HALO + 4, :],
        far[HALO : HALO + 4, :],
        items[0:12, :],
        mate_items[0:12, :],
        far[start : start + 12, :],
        far[start + 16 : start + 28, :],
        following[0:12, :],
    ]
    pack[...] = jnp.concatenate(parts, axis=0)


def relay_kernel(dev, got, send):
    column = dev[0] % 32
    level = dev[0] // 32
    dots = jnp.sum(got[:, 0:8, :], axis=0)
    first, last = column == 0, column == 31
    left = got[(column + 31) % 32, 4:8, :]
    right = got[(column + 1) % 32, 4:8, :]
    near = got[column, 4:8, :] + pick(first, 0.0, left) + pick(last, 0.0, right)
    side = 4 * (1 - level // 4)
    crossing = pick(first, left, pick(last, right, 0.0))
    goal = side + (level + jnp.where(first, 1, jnp.where(last, 3, 0))) % 4
    send[...] = jnp.broadcast_to(jnp.where(iota(0, (8, W)) == 0, dots, 0.0)[None], (8, 8, W))
    send[level ^ 4, 4:8, :] = near

    @pl.when(jnp.logical_or(first, last))
    def _():
        send[goal, 4:8, :] = crossing


def final_kernel(theta_v, field, ui, ue, ki, ke, rows, got, inc, res, inc_s, res_s, work, sems):
    theta = theta_v[0:1, :]
    block = jnp.sum(got[...], axis=0)
    row = block[0:1, :]
    lane1 = iota(1, (1, W))

    def total(k):
        value = jnp.sum(jnp.where(lane1 == k, row, 0.0), axis=1, keepdims=True)
        return jnp.broadcast_to(value, (1, W))

    norm0, curve0, zz, zaz = total(0), total(1), total(2), total(3)
    step0 = norm0 / curve0
    lead = 1.0 - step0 * theta
    norm1 = step0 * step0 * zz - lead * lead * norm0
    rz = curve0 - theta * norm0
    zw = zz + theta * rz
    a = lead + norm1 / norm0
    curve1 = a * a * curve0 - 2.0 * a * step0 * zw + step0 * step0 * zaz
    step1 = norm1 / curve1
    both = step0 + step1 * a
    cross = step1 * step0
    keep = 1.0 - theta * both
    work[0:48, :] = cross * rows[0:48, :]
    for x in range(PLANES):
        j = 4 * (8 + x)
        work[j + 1 : j + 2, :] = work[j + 1 : j + 2, :] - both * rows[49 + 4 * x : 50 + 4 * x, :]
        work[j + 2 : j + 3, :] = (
            work[j + 2 : j + 3, :]
            - both * rows[50 + 4 * x : 51 + 4 * x, :]
            + cross * block[4 + x : 5 + x]
        )
    work[48:64, :] = -cross * rows[48:64, :]
    work[64:W, :] = jnp.zeros((W - 64, W), F32)
    work[...] = work[...].T
    lane = iota(1, (BLOCK, W))
    rim = jnp.logical_or(lane < 2, lane >= W - 2)

    def copies(c, x):
        return [
            pltpu.make_async_copy(source.at[c, x], target.at[c, x], sems.at[i, c, x])
            for i, (source, target) in enumerate(((inc_s, inc), (res_s, res)))
        ]

    def body(i, _):
        for v_from, k_from, x in ((ue, ke, 3 * i), (ui, ki, 1 + i)):
            for c in range(3):

                def block_of(b, _):
                    rows_y = pl.ds(pl.multiple_of(b * BLOCK, BLOCK), BLOCK)
                    columns = work[rows_y, :]

                    def on_rim(q):
                        return jnp.where(rim, pltpu.roll(columns, W - 2 - 4 * q, 1), 0.0)

                    r, v, k = field[c, x, rows_y, :], v_from[c, i, rows_y, :], k_from[c, i, rows_y, :]
                    grown = both * r - cross * v
                    inc_s[c, x, rows_y, :] = grown + on_rim(12 + x) if c == 2 else grown
                    res_s[c, x, rows_y, :] = keep * r - both * v + (cross * k + on_rim(4 * c + x))
                    return 0

                lax.fori_loop(0, W // BLOCK, block_of, 0, unroll=True)
                for copy in copies(c, x):
                    copy.start()
        return 0

    lax.fori_loop(0, 2, body, 0)
    for x in range(PLANES):
        for c in range(3):
            for copy in copies(c, x):
                copy.wait()


def pairs(f):
    return [(i, f(i) % 256) for i in range(256)]


MATE = pairs(lambda i: i ^ 1)
FAR = pairs(lambda i: i + 1 if i % 2 else i - 1)
CROSS = pairs(lambda i: i ^ 128)
PLANE_GROUPS = [[32 * a + b for b in range(32)] for a in range(8)]
COLUMN_GROUPS = [[32 * a + b for a in range(8)] for b in range(32)]


def swap(x, table):
    return lax.ppermute(x, "slab", table)


def exchange(x, groups):
    return lax.all_to_all(x, "slab", 0, 0, tiled=True, axis_index_groups=groups)


def local(rhs, stiff, stencil, dual, mortar, partner, active):
    dev = lax.axis_index("slab").astype(jnp.int32).reshape(1)
    half = (3, 2, W, W)
    shape = rhs.shape
    stage = 8000000
    flat = f32(16, W)

    def whole(n):
        return [vmem()] * n

    def dma(*dims):
        return pltpu.SemaphoreType.DMA(dims)

    st = stencil.reshape(-1)
    field, a_mate, a_far, r_rows = call(
        load_kernel,
        "load",
        [smem(), vmem()],
        (f32(*shape), f32(HALO + 8, W), f32(HALO + 8, W), f32(8, W)),
    )(dev, rhs)
    g_far = swap(a_far, FAR)
    g_mate = swap(a_mate, MATE)
    ui, dots_ui, theta, stiff_v, mortar_v, dual_v, meta = call(
        inner_first_kernel,
        "inner_first",
        [smem()] * 4 + whole(2) + [anywhere()] * 2,
        (
            f32(*half),
            flat,
            f32(8, W),
            f32(PLANES, W, W),
            jax.ShapeDtypeStruct(mortar.shape, mortar.dtype),
            f32(PLANES, W),
            jax.ShapeDtypeStruct((32,), jnp.int32),
        ),
        [pltpu.VMEM((3, 12, W, W), F32), dma(2)],
        stage,
        out_specs=(vmem(),) * 6 + (smem(),),
    )(dev, st, partner, active, field, dual, stiff, mortar)
    own_faces = jnp.concatenate([a_mate[HALO : HALO + 4], g_mate[HALO : HALO + 4], g_far[HALO : HALO + 4]])
    own_faces, ui = lax.optimization_barrier((own_faces, ui))
    faces = swap(own_faces, CROSS)
    ue, dots_ue, b_mate, b_far = call(
        edge_first_kernel,
        "edge_first",
        [smem(), smem()] + whole(5),
        (f32(*half), flat, f32(HALO + 8, W), f32(HALO + 8, W)),
        [pltpu.VMEM((3, 18, W, W), F32)],
        stage,
    )(dev, st, field, g_mate, g_far, stiff_v, ui)
    faces, b_mate, b_far = lax.optimization_barrier((faces, b_mate, b_far))
    items, dots_c = call(
        contact0_kernel,
        "contact0",
        [smem()] + whole(5),
        (f32(16, W), f32(8, W)),
        [pltpu.VMEM((16, W), F32), pltpu.VMEM((24, W), F32)],
    )(meta, faces, g_far, r_rows, dual_v, mortar_v)
    u_rows = b_mate[HALO : HALO + 8]
    h_mate = swap(b_mate, MATE)
    mate_items = swap(items, MATE)
    h_far = swap(jnp.concatenate([b_far, items, mate_items[0:12]]), FAR)
    ki, dots_ki, stiff_rows, coefs = call(
        inner_second_kernel,
        "inner_second",
        [smem()] + whole(3),
        (f32(*half), flat, f32(8, W), f32(88, W)),
        [pltpu.VMEM((3, 12, W, W), F32)],
        stage,
    )(st, ui, ue, stiff_v)
    h_far, ki = lax.optimization_barrier((h_far, ki))
    h_next = swap(h_far[HALO + 8 : HALO + 20], MATE)
    pack = call(gather_kernel, "gather", whole(6), f32(72, W))(u_rows, h_mate, mate_items, h_far, h_next, items)
    cross = swap(pack, CROSS)
    ke, dots_ke, k_rows = call(
        edge_second_kernel,
        "edge_second",
        [smem(), smem()] + whole(6),
        (f32(*half), flat, f32(8, W)),
        [pltpu.VMEM((3, 18, W, W), F32)],
        stage,
    )(dev, st, ui, ue, h_mate, h_far, stiff_v, ki)
    send, rows = call(
        join_kernel,
        "join",
        [smem()] + whole(16),
        (f32(32, 8, W), f32(64, W)),
        [pltpu.VMEM((16, W), F32), pltpu.VMEM((16, W), F32), pltpu.VMEM((24, W), F32)],
    )(
        meta, coefs, mate_items, h_far, pack, cross, items, stiff_rows,
        u_rows, k_rows, dual_v, mortar_v, dots_ui, dots_ue, dots_c, dots_ki, dots_ke,
    )
    got = exchange(send, PLANE_GROUPS)
    relayed = call(relay_kernel, "relay", [smem(), vmem()], f32(8, 8, W))(dev, got)
    sums = exchange(relayed, COLUMN_GROUPS)
    return call(
        final_kernel,
        "final",
        whole(8),
        (f32(*shape), f32(*shape)),
        [pltpu.VMEM(shape, F32), pltpu.VMEM(shape, F32), pltpu.VMEM((W, W), F32), dma(2, 3, 4)],
        out_specs=(anywhere(), anywhere()),
    )(theta, field, ui, ue, ki, ke, rows, sums)


def solution(mesh):
    placed = (
        P(None, "slab", None, None),
        P("slab", None, None),
        P(),
        P("slab", None),
        P("slab", None, None, None),
        P("slab", None),
        P("slab"),
    )
    return jax.shard_map(
        local,
        mesh=mesh,
        in_specs=placed,
        out_specs=(P(None, "slab", None, None), P(None, "slab", None, None)),
        check_vma=False,
    )
```

```python
import functools
import jax
import jax.numpy as jnp
from jax import lax
from jax.experimental import pallas as pl
from jax.experimental.pallas import tpu as pltpu
from jax.sharding import PartitionSpec as P

F32 = jnp.float32
VMEM_LIMIT = 24 * 1024 * 1024
W = 128
PLANES = 4
HALO = 3 * W


def vmem():
    return pl.BlockSpec(memory_space=pltpu.VMEM)


def smem():
    return pl.BlockSpec(memory_space=pltpu.SMEM)


def f32(*shape):
    return jax.ShapeDtypeStruct(shape, F32)


def anywhere():
    return pl.BlockSpec(memory_space=pl.ANY)


def call(kernel, name, ins, outs, scratch=(), cost=1000000, out_specs=None):
    return pl.pallas_call(
        kernel,
        out_shape=outs,
        in_specs=ins,
        out_specs=jax.tree.map(lambda _: vmem(), outs) if out_specs is None else out_specs,
        scratch_shapes=list(scratch),
        compiler_params=pltpu.CompilerParams(vmem_limit_bytes=VMEM_LIMIT),
        cost_estimate=pl.CostEstimate(flops=1000, bytes_accessed=cost, transcendentals=0),
        name=name,
    )


def iota(axis, shape=(W, W)):
    return lax.broadcasted_iota(jnp.int32, shape, axis)


def coefficient(st, k, c, e):
    return st[9 * k + 3 * c + e]


def shift_of(st):
    trace = coefficient(st, 13, 0, 0) + coefficient(st, 13, 1, 1) + coefficient(st, 13, 2, 2)
    return trace * F32(1.0 / 3.0) + F32(2.125)


def face_rows(planes):
    lane = iota(1)
    block = jnp.zeros((W, W), F32)
    for k, plane in enumerate(planes):
        moved = pltpu.roll(plane, 2 * k + 1, 1)
        block = jnp.where(lane // 2 == k, moved, block)
    rows = block.T[0:8, :]
    order = [1, 3, 5, 7, 0, 2, 4, 6]
    return jnp.concatenate([rows[i : i + 1] for i in order], axis=0)


def pick(flag, yes, no):
    return jnp.where(flag, yes, no)


def pick(flag, yes, no):
    return jnp.where(flag, yes, no)


def place_of(dev):
    odd = dev[0] % 2 == 1
    place = dev[0] % 128
    return odd, place


def is_cut(place):
    return jnp.logical_or(place == 63, place == 64)


def is_wrap(place):
    return jnp.logical_or(place == 0, place == 127)


def load_kernel(dev, rhs, field, mate, far, faces):
    odd, _ = place_of(dev)
    for c in range(3):
        low, high = rhs[c, 0], rhs[c, PLANES - 1]
        mate[c * W : (c + 1) * W, :] = pick(odd, low, high)
        far[c * W : (c + 1) * W, :] = pick(odd, high, low)
    rows = face_rows([rhs[2, t] for t in range(PLANES)])
    faces[...] = rows
    mate[HALO : HALO + 8, :] = rows
    far[HALO : HALO + 8, :] = rows
    field[...] = rhs[...]


BLOCK = 32


def fill_shifted(s, planes):
    row = iota(0)

    def body(c, _):
        for x in range(planes):
            i = c * planes + x
            v = s[1, i]
            s[0, i] = jnp.where(row == 0, 0.0, pltpu.roll(v, 1, 0))
            s[2, i] = jnp.where(row == W - 1, 0.0, pltpu.roll(v, W - 1, 0))
        return 0

    lax.fori_loop(0, 3, body, 0)


def sweep(s, st, planes, centre, emit):
    lane = iota(1, (BLOCK, W))
    steps = W // BLOCK

    def body(it, dots):
        x = it // steps
        y = pl.multiple_of((it % steps) * BLOCK, BLOCK)
        rows = pl.ds(y, BLOCK)
        acc = [[None] * 3 for _ in range(3)]
        for dx in range(3):
            for dy in range(3):
                for e in range(3):
                    v = s[dy, e * planes + centre(x) + dx - 1, rows, :]
                    for dz in range(3):
                        for c in range(3):
                            term = coefficient(st, 9 * dx + 3 * dy + dz, c, e) * v
                            acc[dz][c] = term if acc[dz][c] is None else acc[dz][c] + term
        out = []
        for c in range(3):
            below = jnp.where(lane == 0, 0.0, pltpu.roll(acc[0][c], 1, 1))
            above = jnp.where(lane == W - 1, 0.0, pltpu.roll(acc[2][c], W - 1, 1))
            out.append(acc[1][c] + (below + above))
        values = [s[1, c * planes + centre(x), rows, :] for c in range(3)]
        return emit(x, rows, out, values, dots)

    zero = jnp.zeros((8, W), F32)
    return lax.fori_loop(0, 2 * steps, body, (zero, zero))


def fold(v):
    return jnp.sum(v.reshape(BLOCK // 8, 8, W), axis=0)


def emitter(target, stiff, plane, theta):
    def emit(x, rows, out, values, sums):
        square, energy = sums
        k = stiff[plane(x), rows, :]
        for c in range(3):
            v = values[c]
            image = out[c] + k * v
            target[c, x, rows, :] = image if theta is None else image - theta * v
            square += fold(v * v)
            energy += fold(v * image)
        return square, energy

    return emit


def store_dots(dots, sums):
    dots[0:8, :] = sums[0]
    dots[8:16, :] = sums[1]


FACE_TERMS = [(3 * j + dz, c) for dz in range(3) for c in range(3) for j in range(9)]


def inner(x):
    return x + 1


def outer(x):
    return 3 * x


def inner_first_kernel(
    st, partner, active, field, dual, stiff, mortar,
    ui, dots, theta, stiff_v, mortar_v, dual_v, masks, s, sems,
):
    stiff_copy = pltpu.make_async_copy(stiff, stiff_v, sems.at[0])
    mortar_copy = pltpu.make_async_copy(mortar, mortar_v, sems.at[1])
    stiff_copy.start()
    mortar_copy.start()
    dual_v[...] = dual[...]
    masks[...] = jnp.zeros(masks.shape, F32)
    for t in range(PLANES):
        for slot in range(3):
            for k in range(4):
                at = 8 * (4 * slot + k) + t
                chosen = jnp.where(partner[t, slot] % 4 == k, F32(1.0), F32(0.0))
                masks[at : at + 1, :] = jnp.full((1, W), chosen, F32)
        masks[96 + t : 97 + t, :] = jnp.full((1, W), F32(4.0) * active[t].astype(F32), F32)
    for c in range(3):
        for x in range(PLANES):
            s[1, c * 4 + x] = field[c, x]
    fill_shifted(s, 4)
    theta[...] = jnp.full((8, W), shift_of(st), F32)
    stiff_copy.wait()
    store_dots(dots, sweep(s, st, 4, inner, emitter(ui, stiff_v, inner, shift_of(st))))
    mortar_copy.wait()


def fill_halo(dev, s, mate, far, edge_planes, inner_planes):
    odd, place = place_of(dev)
    cut = is_cut(place)
    for c in range(3):
        a = mate[c * W : (c + 1) * W, :]
        b = pick(cut, 0.0, far[c * W : (c + 1) * W, :])
        s[1, c * 6] = pick(odd, a, b)
        s[1, c * 6 + 5] = pick(odd, b, a)
        s[1, c * 6 + 1] = edge_planes(c, 0)
        s[1, c * 6 + 4] = edge_planes(c, 1)
        s[1, c * 6 + 2] = inner_planes(c, 0)
        s[1, c * 6 + 3] = inner_planes(c, 1)
    fill_shifted(s, 6)


def centre6(x):
    return 3 * x + 1


def edge_first_kernel(dev, st, field, mate, far, stiff, ui, ue, dots, to_mate, to_far, s):
    odd, _ = place_of(dev)
    fill_halo(dev, s, mate, far, lambda c, i: field[c, 3 * i], lambda c, i: field[c, 1 + i])
    store_dots(dots, sweep(s, st, 6, centre6, emitter(ue, stiff, outer, shift_of(st))))
    for c in range(3):
        low, high = ue[c, 0], ue[c, 1]
        to_mate[c * W : (c + 1) * W, :] = pick(odd, low, high)
        to_far[c * W : (c + 1) * W, :] = pick(odd, high, low)
    rows = face_rows([ue[2, 0], ui[2, 0], ui[2, 1], ue[2, 1]])
    to_mate[HALO : HALO + 8, :] = rows
    to_far[HALO : HALO + 8, :] = rows


def inner_second_kernel(st, ui, ue, stiff, ki, dots, stiff_rows, coefs, s):
    for c in range(3):
        s[1, c * 4] = ue[c, 0]
        s[1, c * 4 + 1] = ui[c, 0]
        s[1, c * 4 + 2] = ui[c, 1]
        s[1, c * 4 + 3] = ue[c, 1]
    fill_shifted(s, 4)
    store_dots(dots, sweep(s, st, 4, inner, emitter(ki, stiff, inner, None)))
    stiff_rows[...] = face_rows([stiff[t] for t in range(PLANES)])
    for i, (k, c) in enumerate(FACE_TERMS):
        coefs[i : i + 1, :] = jnp.full((1, W), coefficient(st, k, c, 2), F32)


def edge_second_kernel(dev, st, ui, ue, mate, far, stiff, ki, ke, dots, rows, s):
    fill_halo(dev, s, mate, far, lambda c, i: ue[c, i], lambda c, i: ui[c, i])
    store_dots(dots, sweep(s, st, 6, centre6, emitter(ke, stiff, outer, None)))
    rows[...] = face_rows([ke[2, 0], ki[2, 0], ki[2, 1], ke[2, 1]])


def thirds(v):
    a = v.astype(jnp.bfloat16).astype(F32)
    rest = v - a
    b = rest.astype(jnp.bfloat16).astype(F32)
    return jnp.concatenate([a, b, rest - b, jnp.zeros_like(a)], axis=0).astype(jnp.bfloat16)


def contact(masks, slave, table, dual, mortar, back):
    parts = []
    for s in range(3):
        chosen = None
        for k in range(4):
            j = 4 * s + k
            term = masks[8 * j : 8 * j + PLANES, :] * table[j : j + 1, :]
            chosen = term if chosen is None else chosen + term
        parts.append(thirds(chosen))
    left = jnp.concatenate(parts, axis=1)
    blocks = [jnp.concatenate([mortar[t, s] for s in range(3)], axis=1) for t in range(PLANES)]
    pulled = []
    for t in range(PLANES):
        got = lax.dot_general(
            left, blocks[t], (((1,), (1,)), ((), ())), preferred_element_type=F32
        )
        pulled.append(got[t : t + 1] + (got[4 + t : 5 + t] + got[8 + t : 9 + t]))
    gap = dual * slave - jnp.concatenate(pulled, axis=0)
    push = masks[96 : 96 + PLANES, :] * gap
    left = thirds(push)
    rows = []
    for t in range(PLANES):
        got = jnp.dot(left, blocks[t], preferred_element_type=F32)
        rows.append(got[t : t + 1] + (got[4 + t : 5 + t] + got[8 + t : 9 + t]))
    for s in range(3):
        slot = jnp.concatenate([row[:, s * W : (s + 1) * W] for row in rows], axis=0)
        for k in range(4):
            j = 4 * s + k
            back[j : j + 1, :] = -jnp.sum(masks[8 * j : 8 * j + PLANES, :] * slot, axis=0, keepdims=True)
    return push * gap, dual * push


def pad8(rows):
    return jnp.concatenate([rows, jnp.zeros((8 - PLANES, W), F32)], axis=0)


def contact0_kernel(dev, masks, faces, far, r_rows, dual, mortar, items, dots, table):
    odd, place = place_of(dev)
    own, mate = faces[0:4, :], faces[4:8, :]
    other = pick(is_wrap(place), far[HALO : HALO + 4, :], faces[8:12, :])
    table[0:4, :] = pick(odd, mate, other)
    table[4:8, :] = own
    table[8:12, :] = pick(odd, other, mate)
    energy, pushed = contact(masks, r_rows[4:8, :], table, dual[...], mortar, items)
    items[12:16, :] = pushed
    dots[...] = pad8(energy)


def lists(pack, other, odd, swap_far, swap_next):
    own = pack[12:24, :]
    mate = pack[24:36, :]
    far = pick(swap_far, other[36:48, :], pack[36:48, :])
    far_mate = pick(swap_far, other[48:60, :], pack[48:60, :])
    mate_far = pick(swap_next, other[60:72, :], pack[60:72, :])
    m1 = pick(odd, mate, far)
    m2 = pick(odd, mate_far, far_mate)
    p1 = pick(odd, far, mate)
    p2 = pick(odd, far_mate, mate_far)
    return (
        m2[8:12] + m1[4:8] + own[0:4],
        m1[8:12] + own[4:8] + p1[0:4],
        own[8:12] + p1[4:8] + p2[0:4],
    )


def join_kernel(
    dev, masks, coefs, mate_items, far, pack, cross, items, stiff_rows, u_rows, k_rows,
    dual, mortar, dots_ui, dots_ue, dots_c, dots_ki, dots_ke,
    send, rows, table, back,
):
    odd, place = place_of(dev)
    cut, swap_far = is_cut(place), is_wrap(place)
    even = jnp.logical_not(odd)
    swap_next = jnp.logical_or(place == 1, place == 126)
    slave = lists(pack, cross, odd, swap_far, swap_next)
    master = lists(cross, pack, odd, swap_far, swap_next)
    other = pick(swap_far, pack[8:12, :], cross[8:12, :])
    table[0:4, :] = pick(odd, cross[4:8, :], other) + slave[0]
    table[4:8, :] = cross[0:4, :] + slave[1]
    table[8:12, :] = pick(odd, other, cross[4:8, :]) + slave[2]

    energy, pushed = contact(masks, u_rows[4:8, :] + items[12:16, :], table, dual[...], mortar, back)

    low = jnp.logical_and(cut, even)
    high = jnp.logical_and(cut, odd)
    own_total, own_push = master[1], items[12:16, :]
    before = pick(place == 0, slave[0], master[0])[3:4]
    after = pick(place == 127, slave[2], master[2])[0:1]
    mate_push = mate_items[12:16, :]
    far_push = far[HALO + 20 : HALO + 24, :]
    push_before = pick(odd, mate_push, far_push)[3:4]
    push_after = pick(odd, far_push, mate_push)[0:1]
    totals = jnp.concatenate([pick(low, 0.0, before), own_total, pick(high, 0.0, after)], axis=0)
    pushes = jnp.concatenate([pick(low, 0.0, push_before), own_push, pick(high, 0.0, push_after)], axis=0)
    lane = iota(1, (PLANES, W))

    def shifts(rows6):
        out = []
        for dx in range(3):
            v = rows6[dx : dx + PLANES]
            out.append(
                (
                    jnp.where(lane == 0, 0.0, pltpu.roll(v, 1, 1)),
                    v,
                    jnp.where(lane == W - 1, 0.0, pltpu.roll(v, W - 1, 1)),
                )
            )
        return out

    lines = {}
    for k, (rows6, dz) in enumerate(((totals, 1), (totals, 0), (pushes, 2), (pushes, 1))):
        moved = shifts(rows6)
        for c in range(3):
            total = None
            for dx in range(3):
                for dy in range(3):
                    at = FACE_TERMS.index((9 * dx + 3 * dy + dz, c))
                    term = coefs[at : at + 1, :] * moved[dx][dy]
                    total = term if total is None else total + term
            lines[k, c] = total
    lines[0, 2] = lines[0, 2] + stiff_rows[0:4, :] * own_total
    lines[3, 2] = lines[3, 2] + stiff_rows[4:8, :] * own_push
    bend = lines[3, 2]
    lines[3, 2] = bend + pushed
    for c in range(3):
        for x in range(PLANES):
            for i, k in enumerate((2, 3, 0, 1)):
                j = 4 * (4 * c + x) + i
                rows[j : j + 1, :] = lines[k, c][x : x + 1]
    rows[48:64, :] = jnp.zeros((16, W), F32)
    for x in range(PLANES):
        rows[4 * x + 49 : 4 * x + 50, :] = own_push[x : x + 1]
        rows[4 * x + 50 : 4 * x + 51, :] = own_total[x : x + 1]
    face = own_total * u_rows[0:4, :] + own_push * u_rows[4:8, :]
    square = own_total * own_total + own_push * own_push
    image = own_total * (2.0 * k_rows[0:4, :] + lines[0, 2]) + own_push * (2.0 * k_rows[4:8, :] + bend)
    values = (
        dots_ui[0:8, :] + dots_ue[0:8, :],
        dots_ui[8:16, :] + dots_ue[8:16, :] + dots_c[...],
        dots_ki[0:8, :] + dots_ke[0:8, :],
        dots_ki[8:16, :] + dots_ke[8:16, :] + pad8(energy),
    )
    extra = (None, None, 2.0 * face + square, image)
    dot_rows = []
    for value, more in zip(values, extra):
        row = jnp.sum(value, axis=0, keepdims=True)
        if more is not None:
            row = row + jnp.sum(more, axis=0, keepdims=True)
        dot_rows.append(row)
    block = jnp.concatenate(dot_rows + [jnp.zeros((4, W), F32)], axis=0)
    send[...] = jnp.broadcast_to(block[None], (32, 8, W))
    column = dev[0] % 32
    send[(column + 31) % 32, 4:8, :] = back[0:4, :]
    send[column, 4:8, :] = back[4:8, :]
    send[(column + 1) % 32, 4:8, :] = back[8:12, :]


def gather_kernel(u_rows, mate, mate_items, far, following, items, pack):
    start = HALO + 8
    parts = [
        u_rows[0:4, :],
        mate[HALO : HALO + 4, :],
        far[HALO : HALO + 4, :],
        items[0:12, :],
        mate_items[0:12, :],
        far[start : start + 12, :],
        far[start + 16 : start + 28, :],
        following[0:12, :],
    ]
    pack[...] = jnp.concatenate(parts, axis=0)


def relay_kernel(dev, got, send):
    column = dev[0] % 32
    level = dev[0] // 32
    dots = jnp.sum(got[:, 0:8, :], axis=0)
    first, last = column == 0, column == 31
    left = got[(column + 31) % 32, 4:8, :]
    right = got[(column + 1) % 32, 4:8, :]
    near = got[column, 4:8, :] + pick(first, 0.0, left) + pick(last, 0.0, right)
    side = 4 * (1 - level // 4)
    crossing = pick(first, left, pick(last, right, 0.0))
    goal = side + (level + jnp.where(first, 1, jnp.where(last, 3, 0))) % 4
    send[...] = jnp.broadcast_to(jnp.where(iota(0, (8, W)) < 4, dots, 0.0)[None], (8, 8, W))
    send[level ^ 4, 4:8, :] = near

    @pl.when(jnp.logical_or(first, last))
    def _():
        send[goal, 4:8, :] = crossing


def final_kernel(theta_v, field, ui, ue, ki, ke, rows, got, inc, res, inc_s, res_s, work, sems):
    theta = theta_v[0:1, :]
    block = jnp.sum(got[...], axis=0)

    def total(k):
        value = jnp.sum(block[k : k + 1, :], axis=1, keepdims=True)
        return jnp.broadcast_to(value, (1, W))

    norm0, curve0, zz, zaz = total(0), total(1), total(2), total(3)
    step0 = norm0 / curve0
    lead = 1.0 - step0 * theta
    norm1 = step0 * step0 * zz - lead * lead * norm0
    rz = curve0 - theta * norm0
    zw = zz + theta * rz
    a = lead + norm1 / norm0
    curve1 = a * a * curve0 - 2.0 * a * step0 * zw + step0 * step0 * zaz
    step1 = norm1 / curve1
    both = step0 + step1 * a
    cross = step1 * step0
    keep = 1.0 - theta * both
    work[0:48, :] = cross * rows[0:48, :]
    for x in range(PLANES):
        j = 4 * (8 + x)
        work[j + 1 : j + 2, :] = work[j + 1 : j + 2, :] - both * rows[49 + 4 * x : 50 + 4 * x, :]
        work[j + 2 : j + 3, :] = (
            work[j + 2 : j + 3, :]
            - both * rows[50 + 4 * x : 51 + 4 * x, :]
            + cross * block[4 + x : 5 + x]
        )
    work[48:64, :] = -cross * rows[48:64, :]
    work[64:W, :] = jnp.zeros((W - 64, W), F32)
    work[...] = work[...].T
    lane = iota(1, (BLOCK, W))
    rim = jnp.logical_or(lane < 2, lane >= W - 2)

    def copies(c, x):
        return [
            pltpu.make_async_copy(source.at[c, x], target.at[c, x], sems.at[i, c, x])
            for i, (source, target) in enumerate(((inc_s, inc), (res_s, res)))
        ]

    def body(i, _):
        for v_from, k_from, x in ((ue, ke, 3 * i), (ui, ki, 1 + i)):
            for c in range(3):

                def block_of(b, _):
                    rows_y = pl.ds(pl.multiple_of(b * BLOCK, BLOCK), BLOCK)
                    columns = work[rows_y, :]

                    def on_rim(q):
                        return jnp.where(rim, pltpu.roll(columns, W - 2 - 4 * q, 1), 0.0)

                    r, v, k = field[c, x, rows_y, :], v_from[c, i, rows_y, :], k_from[c, i, rows_y, :]
                    grown = both * r - cross * v
                    inc_s[c, x, rows_y, :] = grown + on_rim(12 + x) if c == 2 else grown
                    res_s[c, x, rows_y, :] = keep * r - both * v + (cross * k + on_rim(4 * c + x))
                    return 0

                lax.fori_loop(0, W // BLOCK, block_of, 0, unroll=True)
                for copy in copies(c, x):
                    copy.start()
        return 0

    lax.fori_loop(0, 2, body, 0)
    for x in range(PLANES):
        for c in range(3):
            for copy in copies(c, x):
                copy.wait()


def pairs(f):
    return [(i, f(i) % 256) for i in range(256)]


MATE = pairs(lambda i: i ^ 1)
FAR = pairs(lambda i: i + 1 if i % 2 else i - 1)
CROSS = pairs(lambda i: i ^ 128)
PLANE_GROUPS = [[32 * a + b for b in range(32)] for a in range(8)]
COLUMN_GROUPS = [[32 * a + b for a in range(8)] for b in range(32)]


def swap(x, table):
    return lax.ppermute(x, "slab", table)


def exchange(x, groups):
    return lax.all_to_all(x, "slab", 0, 0, tiled=True, axis_index_groups=groups)


def local(rhs, stiff, stencil, dual, mortar, partner, active):
    dev = lax.axis_index("slab").astype(jnp.int32).reshape(1)
    half = (3, 2, W, W)
    shape = rhs.shape
    stage = 8000000
    flat = f32(16, W)

    def whole(n):
        return [vmem()] * n

    def dma(*dims):
        return pltpu.SemaphoreType.DMA(dims)

    st = stencil.reshape(-1)
    field, a_mate, a_far, r_rows = call(
        load_kernel,
        "load",
        [smem(), vmem()],
        (f32(*shape), f32(HALO + 8, W), f32(HALO + 8, W), f32(8, W)),
    )(dev, rhs)
    g_far = swap(a_far, FAR)
    g_mate = swap(a_mate, MATE)
    ui, dots_ui, theta, stiff_v, mortar_v, dual_v, masks = call(
        inner_first_kernel,
        "inner_first",
        [smem()] * 3 + whole(2) + [anywhere()] * 2,
        (
            f32(*half),
            flat,
            f32(8, W),
            f32(PLANES, W, W),
            jax.ShapeDtypeStruct(mortar.shape, mortar.dtype),
            f32(PLANES, W),
            f32(104, W),
        ),
        [pltpu.VMEM((3, 12, W, W), F32), dma(2)],
        stage,
    )(st, partner, active, field, dual, stiff, mortar)
    own_faces = jnp.concatenate([a_mate[HALO : HALO + 4], g_mate[HALO : HALO + 4], g_far[HALO : HALO + 4]])
    own_faces, ui = lax.optimization_barrier((own_faces, ui))
    faces = swap(own_faces, CROSS)
    ue, dots_ue, b_mate, b_far = call(
        edge_first_kernel,
        "edge_first",
        [smem(), smem()] + whole(5),
        (f32(*half), flat, f32(HALO + 8, W), f32(HALO + 8, W)),
        [pltpu.VMEM((3, 18, W, W), F32)],
        stage,
    )(dev, st, field, g_mate, g_far, stiff_v, ui)
    faces, b_mate, b_far = lax.optimization_barrier((faces, b_mate, b_far))
    items, dots_c = call(
        contact0_kernel,
        "contact0",
        [smem()] + whole(6),
        (f32(16, W), f32(8, W)),
        [pltpu.VMEM((16, W), F32)],
    )(dev, masks, faces, g_far, r_rows, dual_v, mortar_v)
    u_rows = b_mate[HALO : HALO + 8]
    h_mate = swap(b_mate, MATE)
    mate_items = swap(items, MATE)
    h_far = swap(jnp.concatenate([b_far, items, mate_items[0:12]]), FAR)
    ki, dots_ki, stiff_rows, coefs = call(
        inner_second_kernel,
        "inner_second",
        [smem()] + whole(3),
        (f32(*half), flat, f32(8, W), f32(88, W)),
        [pltpu.VMEM((3, 12, W, W), F32)],
        stage,
    )(st, ui, ue, stiff_v)
    h_far, ki = lax.optimization_barrier((h_far, ki))
    h_next = swap(h_far[HALO + 8 : HALO + 20], MATE)
    pack = call(gather_kernel, "gather", whole(6), f32(72, W))(u_rows, h_mate, mate_items, h_far, h_next, items)
    cross = swap(pack, CROSS)
    ke, dots_ke, k_rows = call(
        edge_second_kernel,
        "edge_second",
        [smem(), smem()] + whole(6),
        (f32(*half), flat, f32(8, W)),
        [pltpu.VMEM((3, 18, W, W), F32)],
        stage,
    )(dev, st, ui, ue, h_mate, h_far, stiff_v, ki)
    send, rows = call(
        join_kernel,
        "join",
        [smem()] + whole(17),
        (f32(32, 8, W), f32(64, W)),
        [pltpu.VMEM((16, W), F32), pltpu.VMEM((16, W), F32)],
    )(
        dev, masks, coefs, mate_items, h_far, pack, cross, items, stiff_rows,
        u_rows, k_rows, dual_v, mortar_v, dots_ui, dots_ue, dots_c, dots_ki, dots_ke,
    )
    got = exchange(send, PLANE_GROUPS)
    relayed = call(relay_kernel, "relay", [smem(), vmem()], f32(8, 8, W))(dev, got)
    sums = exchange(relayed, COLUMN_GROUPS)
    return call(
        final_kernel,
        "final",
        whole(8),
        (f32(*shape), f32(*shape)),
        [pltpu.VMEM(shape, F32), pltpu.VMEM(shape, F32), pltpu.VMEM((W, W), F32), dma(2, 3, 4)],
        out_specs=(anywhere(), anywhere()),
    )(theta, field, ui, ue, ki, ke, rows, sums)


def solution(mesh):
    placed = (
        P(None, "slab", None, None),
        P("slab", None, None),
        P(),
        P("slab", None),
        P("slab", None, None, None),
        P("slab", None),
        P("slab"),
    )
    return jax.shard_map(
        local,
        mesh=mesh,
        in_specs=placed,
        out_specs=(P(None, "slab", None, None), P(None, "slab", None, None)),
        check_vma=False,
    )
```

```python
import functools
import jax
import jax.numpy as jnp
from jax import lax
from jax.experimental import pallas as pl
from jax.experimental.pallas import tpu as pltpu
from jax.sharding import PartitionSpec as P

F32 = jnp.float32
VMEM_LIMIT = 24 * 1024 * 1024
W = 128
PLANES = 4
HALO = 3 * W


def vmem():
    return pl.BlockSpec(memory_space=pltpu.VMEM)


def smem():
    return pl.BlockSpec(memory_space=pltpu.SMEM)


def f32(*shape):
    return jax.ShapeDtypeStruct(shape, F32)


def anywhere():
    return pl.BlockSpec(memory_space=pl.ANY)


def call(kernel, name, ins, outs, scratch=(), cost=1000000, out_specs=None):
    return pl.pallas_call(
        kernel,
        out_shape=outs,
        in_specs=ins,
        out_specs=jax.tree.map(lambda _: vmem(), outs) if out_specs is None else out_specs,
        scratch_shapes=list(scratch),
        compiler_params=pltpu.CompilerParams(vmem_limit_bytes=VMEM_LIMIT),
        cost_estimate=pl.CostEstimate(flops=1000, bytes_accessed=cost, transcendentals=0),
        name=name,
    )


def iota(axis, shape=(W, W)):
    return lax.broadcasted_iota(jnp.int32, shape, axis)


def coefficient(st, k, c, e):
    return st[9 * k + 3 * c + e]


def shift_of(st):
    trace = coefficient(st, 13, 0, 0) + coefficient(st, 13, 1, 1) + coefficient(st, 13, 2, 2)
    return trace * F32(1.0 / 3.0) + F32(2.125)


def face_rows(planes):
    lane = iota(1)
    block = jnp.zeros((W, W), F32)
    for k, plane in enumerate(planes):
        moved = pltpu.roll(plane, 2 * k + 1, 1)
        block = jnp.where(lane // 2 == k, moved, block)
    rows = block.T[0:8, :]
    order = [1, 3, 5, 7, 0, 2, 4, 6]
    return jnp.concatenate([rows[i : i + 1] for i in order], axis=0)


def pick(flag, yes, no):
    return jnp.where(flag, yes, no)


def pick(flag, yes, no):
    return jnp.where(flag, yes, no)


def place_of(dev):
    odd = dev[0] % 2 == 1
    place = dev[0] % 128
    return odd, place


def is_cut(place):
    return jnp.logical_or(place == 63, place == 64)


def is_wrap(place):
    return jnp.logical_or(place == 0, place == 127)


def load_kernel(dev, rhs, field, mate, far, faces):
    odd, _ = place_of(dev)
    for c in range(3):
        low, high = rhs[c, 0], rhs[c, PLANES - 1]
        mate[c * W : (c + 1) * W, :] = pick(odd, low, high)
        far[c * W : (c + 1) * W, :] = pick(odd, high, low)
    rows = face_rows([rhs[2, t] for t in range(PLANES)])
    faces[...] = rows
    mate[HALO : HALO + 8, :] = rows
    far[HALO : HALO + 8, :] = rows
    field[...] = rhs[...]


BLOCK = 32


def fill_shifted(s, planes):
    row = iota(0)

    def body(c, _):
        for x in range(planes):
            i = c * planes + x
            v = s[1, i]
            s[0, i] = jnp.where(row == 0, 0.0, pltpu.roll(v, 1, 0))
            s[2, i] = jnp.where(row == W - 1, 0.0, pltpu.roll(v, W - 1, 0))
        return 0

    lax.fori_loop(0, 3, body, 0)


def sweep(s, st, planes, centre, emit):
    lane = iota(1, (BLOCK, W))
    steps = W // BLOCK

    def body(it, dots):
        x = it // steps
        y = pl.multiple_of((it % steps) * BLOCK, BLOCK)
        rows = pl.ds(y, BLOCK)
        acc = [[None] * 3 for _ in range(3)]
        for dx in range(3):
            for dy in range(3):
                for e in range(3):
                    v = s[dy, e * planes + centre(x) + dx - 1, rows, :]
                    for dz in range(3):
                        for c in range(3):
                            term = coefficient(st, 9 * dx + 3 * dy + dz, c, e) * v
                            acc[dz][c] = term if acc[dz][c] is None else acc[dz][c] + term
        out = []
        for c in range(3):
            below = jnp.where(lane == 0, 0.0, pltpu.roll(acc[0][c], 1, 1))
            above = jnp.where(lane == W - 1, 0.0, pltpu.roll(acc[2][c], W - 1, 1))
            out.append(acc[1][c] + (below + above))
        values = [s[1, c * planes + centre(x), rows, :] for c in range(3)]
        return emit(x, rows, out, values, dots)

    zero = jnp.zeros((8, W), F32)
    return lax.fori_loop(0, 2 * steps, body, (zero, zero))


def fold(v):
    return jnp.sum(v.reshape(BLOCK // 8, 8, W), axis=0)


def emitter(target, stiff, plane, theta):
    def emit(x, rows, out, values, sums):
        square, energy = sums
        k = stiff[plane(x), rows, :]
        for c in range(3):
            v = values[c]
            image = out[c] + k * v
            target[c, x, rows, :] = image if theta is None else image - theta * v
            square += fold(v * v)
            energy += fold(v * image)
        return square, energy

    return emit


def store_dots(dots, sums):
    dots[0:8, :] = sums[0]
    dots[8:16, :] = sums[1]


FACE_TERMS = [(3 * j + dz, c) for dz in range(3) for c in range(3) for j in range(9)]


def inner(x):
    return x + 1


def outer(x):
    return 3 * x


def inner_first_kernel(
    st_from, partner, active, field, dual, stiff, mortar,
    ui, dots, theta, stiff_v, mortar_v, dual_v, masks, s, sems, st,
):
    stiff_copy = pltpu.make_async_copy(stiff, stiff_v, sems.at[0])
    mortar_copy = pltpu.make_async_copy(mortar, mortar_v, sems.at[1])
    st_copy = pltpu.make_async_copy(st_from, st, sems.at[2])
    st_copy.start()
    stiff_copy.start()
    mortar_copy.start()
    dual_v[...] = dual[...]
    masks[...] = jnp.zeros(masks.shape, F32)
    for t in range(PLANES):
        for slot in range(3):
            for k in range(4):
                at = 8 * (4 * slot + k) + t
                chosen = jnp.where(partner[t, slot] % 4 == k, F32(1.0), F32(0.0))
                masks[at : at + 1, :] = jnp.full((1, W), chosen, F32)
        masks[96 + t : 97 + t, :] = jnp.full((1, W), F32(4.0) * active[t].astype(F32), F32)
    for c in range(3):
        for x in range(PLANES):
            s[1, c * 4 + x] = field[c, x]
    fill_shifted(s, 4)
    st_copy.wait()
    theta[...] = jnp.full((8, W), shift_of(st), F32)
    stiff_copy.wait()
    store_dots(dots, sweep(s, st, 4, inner, emitter(ui, stiff_v, inner, shift_of(st))))
    mortar_copy.wait()


def fill_halo(dev, s, mate, far, edge_planes, inner_planes):
    odd, place = place_of(dev)
    cut = is_cut(place)
    for c in range(3):
        a = mate[c * W : (c + 1) * W, :]
        b = pick(cut, 0.0, far[c * W : (c + 1) * W, :])
        s[1, c * 6] = pick(odd, a, b)
        s[1, c * 6 + 5] = pick(odd, b, a)
        s[1, c * 6 + 1] = edge_planes(c, 0)
        s[1, c * 6 + 4] = edge_planes(c, 1)
        s[1, c * 6 + 2] = inner_planes(c, 0)
        s[1, c * 6 + 3] = inner_planes(c, 1)
    fill_shifted(s, 6)


def centre6(x):
    return 3 * x + 1


def edge_first_kernel(dev, st_from, field, mate, far, stiff, ui, ue, dots, to_mate, to_far, s, st, sem):
    odd, _ = place_of(dev)
    st_copy = pltpu.make_async_copy(st_from, st, sem)
    st_copy.start()
    fill_halo(dev, s, mate, far, lambda c, i: field[c, 3 * i], lambda c, i: field[c, 1 + i])
    st_copy.wait()
    store_dots(dots, sweep(s, st, 6, centre6, emitter(ue, stiff, outer, shift_of(st))))
    for c in range(3):
        low, high = ue[c, 0], ue[c, 1]
        to_mate[c * W : (c + 1) * W, :] = pick(odd, low, high)
        to_far[c * W : (c + 1) * W, :] = pick(odd, high, low)
    rows = face_rows([ue[2, 0], ui[2, 0], ui[2, 1], ue[2, 1]])
    to_mate[HALO : HALO + 8, :] = rows
    to_far[HALO : HALO + 8, :] = rows


def inner_second_kernel(st_from, ui, ue, stiff, ki, dots, stiff_rows, coefs, s, st, sem):
    st_copy = pltpu.make_async_copy(st_from, st, sem)
    st_copy.start()
    for c in range(3):
        s[1, c * 4] = ue[c, 0]
        s[1, c * 4 + 1] = ui[c, 0]
        s[1, c * 4 + 2] = ui[c, 1]
        s[1, c * 4 + 3] = ue[c, 1]
    fill_shifted(s, 4)
    st_copy.wait()
    store_dots(dots, sweep(s, st, 4, inner, emitter(ki, stiff, inner, None)))
    stiff_rows[...] = face_rows([stiff[t] for t in range(PLANES)])
    for i, (k, c) in enumerate(FACE_TERMS):
        coefs[i : i + 1, :] = jnp.full((1, W), coefficient(st, k, c, 2), F32)


def edge_second_kernel(dev, st_from, ui, ue, mate, far, stiff, ki, ke, dots, rows, s, st, sem):
    st_copy = pltpu.make_async_copy(st_from, st, sem)
    st_copy.start()
    fill_halo(dev, s, mate, far, lambda c, i: ue[c, i], lambda c, i: ui[c, i])
    st_copy.wait()
    store_dots(dots, sweep(s, st, 6, centre6, emitter(ke, stiff, outer, None)))
    rows[...] = face_rows([ke[2, 0], ki[2, 0], ki[2, 1], ke[2, 1]])


def thirds(v):
    a = v.astype(jnp.bfloat16).astype(F32)
    rest = v - a
    b = rest.astype(jnp.bfloat16).astype(F32)
    return jnp.concatenate([a, b, rest - b, jnp.zeros_like(a)], axis=0).astype(jnp.bfloat16)


def contact(masks, slave, table, dual, mortar, back):
    parts = []
    for s in range(3):
        chosen = None
        for k in range(4):
            j = 4 * s + k
            term = masks[8 * j : 8 * j + PLANES, :] * table[j : j + 1, :]
            chosen = term if chosen is None else chosen + term
        parts.append(thirds(chosen))
    left = jnp.concatenate(parts, axis=1)
    blocks = [jnp.concatenate([mortar[t, s] for s in range(3)], axis=1) for t in range(PLANES)]
    pulled = []
    for t in range(PLANES):
        got = lax.dot_general(
            left, blocks[t], (((1,), (1,)), ((), ())), preferred_element_type=F32
        )
        pulled.append(got[t : t + 1] + (got[4 + t : 5 + t] + got[8 + t : 9 + t]))
    gap = dual * slave - jnp.concatenate(pulled, axis=0)
    push = masks[96 : 96 + PLANES, :] * gap
    left = thirds(push)
    rows = []
    for t in range(PLANES):
        got = jnp.dot(left, blocks[t], preferred_element_type=F32)
        rows.append(got[t : t + 1] + (got[4 + t : 5 + t] + got[8 + t : 9 + t]))
    for s in range(3):
        slot = jnp.concatenate([row[:, s * W : (s + 1) * W] for row in rows], axis=0)
        for k in range(4):
            j = 4 * s + k
            back[j : j + 1, :] = -jnp.sum(masks[8 * j : 8 * j + PLANES, :] * slot, axis=0, keepdims=True)
    return push * gap, dual * push


def pad8(rows):
    return jnp.concatenate([rows, jnp.zeros((8 - PLANES, W), F32)], axis=0)


def contact0_kernel(dev, masks, faces, far, r_rows, dual, mortar, items, dots, table):
    odd, place = place_of(dev)
    own, mate = faces[0:4, :], faces[4:8, :]
    other = pick(is_wrap(place), far[HALO : HALO + 4, :], faces[8:12, :])
    table[0:4, :] = pick(odd, mate, other)
    table[4:8, :] = own
    table[8:12, :] = pick(odd, other, mate)
    energy, pushed = contact(masks, r_rows[4:8, :], table, dual[...], mortar, items)
    items[12:16, :] = pushed
    dots[...] = pad8(energy)


def lists(pack, other, odd, swap_far, swap_next):
    own = pack[12:24, :]
    mate = pack[24:36, :]
    far = pick(swap_far, other[36:48, :], pack[36:48, :])
    far_mate = pick(swap_far, other[48:60, :], pack[48:60, :])
    mate_far = pick(swap_next, other[60:72, :], pack[60:72, :])
    m1 = pick(odd, mate, far)
    m2 = pick(odd, mate_far, far_mate)
    p1 = pick(odd, far, mate)
    p2 = pick(odd, far_mate, mate_far)
    return (
        m2[8:12] + m1[4:8] + own[0:4],
        m1[8:12] + own[4:8] + p1[0:4],
        own[8:12] + p1[4:8] + p2[0:4],
    )


def join_kernel(
    dev, masks, coefs, mate_items, far, pack, cross, items, stiff_rows, u_rows, k_rows,
    dual, mortar, dots_ui, dots_ue, dots_c, dots_ki, dots_ke,
    send, rows, table, back,
):
    odd, place = place_of(dev)
    cut, swap_far = is_cut(place), is_wrap(place)
    even = jnp.logical_not(odd)
    swap_next = jnp.logical_or(place == 1, place == 126)
    slave = lists(pack, cross, odd, swap_far, swap_next)
    master = lists(cross, pack, odd, swap_far, swap_next)
    other = pick(swap_far, pack[8:12, :], cross[8:12, :])
    table[0:4, :] = pick(odd, cross[4:8, :], other) + slave[0]
    table[4:8, :] = cross[0:4, :] + slave[1]
    table[8:12, :] = pick(odd, other, cross[4:8, :]) + slave[2]

    energy, pushed = contact(masks, u_rows[4:8, :] + items[12:16, :], table, dual[...], mortar, back)

    low = jnp.logical_and(cut, even)
    high = jnp.logical_and(cut, odd)
    own_total, own_push = master[1], items[12:16, :]
    before = pick(place == 0, slave[0], master[0])[3:4]
    after = pick(place == 127, slave[2], master[2])[0:1]
    mate_push = mate_items[12:16, :]
    far_push = far[HALO + 20 : HALO + 24, :]
    push_before = pick(odd, mate_push, far_push)[3:4]
    push_after = pick(odd, far_push, mate_push)[0:1]
    totals = jnp.concatenate([pick(low, 0.0, before), own_total, pick(high, 0.0, after)], axis=0)
    pushes = jnp.concatenate([pick(low, 0.0, push_before), own_push, pick(high, 0.0, push_after)], axis=0)
    lane = iota(1, (PLANES, W))

    def shifts(rows6):
        out = []
        for dx in range(3):
            v = rows6[dx : dx + PLANES]
            out.append(
                (
                    jnp.where(lane == 0, 0.0, pltpu.roll(v, 1, 1)),
                    v,
                    jnp.where(lane == W - 1, 0.0, pltpu.roll(v, W - 1, 1)),
                )
            )
        return out

    lines = {}
    for k, (rows6, dz) in enumerate(((totals, 1), (totals, 0), (pushes, 2), (pushes, 1))):
        moved = shifts(rows6)
        for c in range(3):
            total = None
            for dx in range(3):
                for dy in range(3):
                    at = FACE_TERMS.index((9 * dx + 3 * dy + dz, c))
                    term = coefs[at : at + 1, :] * moved[dx][dy]
                    total = term if total is None else total + term
            lines[k, c] = total
    lines[0, 2] = lines[0, 2] + stiff_rows[0:4, :] * own_total
    lines[3, 2] = lines[3, 2] + stiff_rows[4:8, :] * own_push
    bend = lines[3, 2]
    lines[3, 2] = bend + pushed
    for c in range(3):
        for x in range(PLANES):
            for i, k in enumerate((2, 3, 0, 1)):
                j = 4 * (4 * c + x) + i
                rows[j : j + 1, :] = lines[k, c][x : x + 1]
    rows[48:64, :] = jnp.zeros((16, W), F32)
    for x in range(PLANES):
        rows[4 * x + 49 : 4 * x + 50, :] = own_push[x : x + 1]
        rows[4 * x + 50 : 4 * x + 51, :] = own_total[x : x + 1]
    face = own_total * u_rows[0:4, :] + own_push * u_rows[4:8, :]
    square = own_total * own_total + own_push * own_push
    image = own_total * (2.0 * k_rows[0:4, :] + lines[0, 2]) + own_push * (2.0 * k_rows[4:8, :] + bend)
    values = (
        dots_ui[0:8, :] + dots_ue[0:8, :],
        dots_ui[8:16, :] + dots_ue[8:16, :] + dots_c[...],
        dots_ki[0:8, :] + dots_ke[0:8, :],
        dots_ki[8:16, :] + dots_ke[8:16, :] + pad8(energy),
    )
    extra = (None, None, 2.0 * face + square, image)
    dot_rows = []
    for value, more in zip(values, extra):
        row = jnp.sum(value, axis=0, keepdims=True)
        if more is not None:
            row = row + jnp.sum(more, axis=0, keepdims=True)
        dot_rows.append(row)
    block = jnp.concatenate(dot_rows + [jnp.zeros((4, W), F32)], axis=0)
    send[...] = jnp.broadcast_to(block[None], (32, 8, W))
    column = dev[0] % 32
    send[(column + 31) % 32, 4:8, :] = back[0:4, :]
    send[column, 4:8, :] = back[4:8, :]
    send[(column + 1) % 32, 4:8, :] = back[8:12, :]


def gather_kernel(u_rows, mate, mate_items, far, following, items, pack):
    start = HALO + 8
    parts = [
        u_rows[0:4, :],
        mate[HALO : HALO + 4, :],
        far[HALO : HALO + 4, :],
        items[0:12, :],
        mate_items[0:12, :],
        far[start : start + 12, :],
        far[start + 16 : start + 28, :],
        following[0:12, :],
    ]
    pack[...] = jnp.concatenate(parts, axis=0)


def relay_kernel(dev, got, send):
    column = dev[0] % 32
    level = dev[0] // 32
    dots = jnp.sum(got[:, 0:8, :], axis=0)
    first, last = column == 0, column == 31
    left = got[(column + 31) % 32, 4:8, :]
    right = got[(column + 1) % 32, 4:8, :]
    near = got[column, 4:8, :] + pick(first, 0.0, left) + pick(last, 0.0, right)
    side = 4 * (1 - level // 4)
    crossing = pick(first, left, pick(last, right, 0.0))
    goal = side + (level + jnp.where(first, 1, jnp.where(last, 3, 0))) % 4
    send[...] = jnp.broadcast_to(jnp.where(iota(0, (8, W)) < 4, dots, 0.0)[None], (8, 8, W))
    send[level ^ 4, 4:8, :] = near

    @pl.when(jnp.logical_or(first, last))
    def _():
        send[goal, 4:8, :] = crossing


def final_kernel(theta_v, field, ui, ue, ki, ke, rows, got, inc, res, inc_s, res_s, work, sems):
    theta = theta_v[0:1, :]
    block = jnp.sum(got[...], axis=0)

    def total(k):
        value = jnp.sum(block[k : k + 1, :], axis=1, keepdims=True)
        return jnp.broadcast_to(value, (1, W))

    norm0, curve0, zz, zaz = total(0), total(1), total(2), total(3)
    step0 = norm0 / curve0
    lead = 1.0 - step0 * theta
    norm1 = step0 * step0 * zz - lead * lead * norm0
    rz = curve0 - theta * norm0
    zw = zz + theta * rz
    a = lead + norm1 / norm0
    curve1 = a * a * curve0 - 2.0 * a * step0 * zw + step0 * step0 * zaz
    step1 = norm1 / curve1
    both = step0 + step1 * a
    cross = step1 * step0
    keep = 1.0 - theta * both
    work[0:48, :] = cross * rows[0:48, :]
    for x in range(PLANES):
        j = 4 * (8 + x)
        work[j + 1 : j + 2, :] = work[j + 1 : j + 2, :] - both * rows[49 + 4 * x : 50 + 4 * x, :]
        work[j + 2 : j + 3, :] = (
            work[j + 2 : j + 3, :]
            - both * rows[50 + 4 * x : 51 + 4 * x, :]
            + cross * block[4 + x : 5 + x]
        )
    work[48:64, :] = -cross * rows[48:64, :]
    work[64:W, :] = jnp.zeros((W - 64, W), F32)
    work[...] = work[...].T
    lane = iota(1, (BLOCK, W))
    rim = jnp.logical_or(lane < 2, lane >= W - 2)

    def copies(c, x):
        return [
            pltpu.make_async_copy(source.at[c, x], target.at[c, x], sems.at[i, c, x])
            for i, (source, target) in enumerate(((inc_s, inc), (res_s, res)))
        ]

    def body(i, _):
        for v_from, k_from, x in ((ue, ke, 3 * i), (ui, ki, 1 + i)):
            for c in range(3):

                def block_of(b, _):
                    rows_y = pl.ds(pl.multiple_of(b * BLOCK, BLOCK), BLOCK)
                    columns = work[rows_y, :]

                    def on_rim(q):
                        return jnp.where(rim, pltpu.roll(columns, W - 2 - 4 * q, 1), 0.0)

                    r, v, k = field[c, x, rows_y, :], v_from[c, i, rows_y, :], k_from[c, i, rows_y, :]
                    grown = both * r - cross * v
                    inc_s[c, x, rows_y, :] = grown + on_rim(12 + x) if c == 2 else grown
                    res_s[c, x, rows_y, :] = keep * r - both * v + (cross * k + on_rim(4 * c + x))
                    return 0

                lax.fori_loop(0, W // BLOCK, block_of, 0, unroll=True)
                for copy in copies(c, x):
                    copy.start()
        return 0

    lax.fori_loop(0, 2, body, 0)
    for x in range(PLANES):
        for c in range(3):
            for copy in copies(c, x):
                copy.wait()


def pairs(f):
    return [(i, f(i) % 256) for i in range(256)]


MATE = pairs(lambda i: i ^ 1)
FAR = pairs(lambda i: i + 1 if i % 2 else i - 1)
CROSS = pairs(lambda i: i ^ 128)
PLANE_GROUPS = [[32 * a + b for b in range(32)] for a in range(8)]
COLUMN_GROUPS = [[32 * a + b for a in range(8)] for b in range(32)]


def swap(x, table):
    return lax.ppermute(x, "slab", table)


def exchange(x, groups):
    return lax.all_to_all(x, "slab", 0, 0, tiled=True, axis_index_groups=groups)


def local(rhs, stiff, stencil, dual, mortar, partner, active):
    dev = lax.axis_index("slab").astype(jnp.int32).reshape(1)
    half = (3, 2, W, W)
    shape = rhs.shape
    stage = 8000000
    flat = f32(16, W)
    flat_st = pltpu.SMEM((243,), F32)

    def whole(n):
        return [vmem()] * n

    def dma(*dims):
        return pltpu.SemaphoreType.DMA(dims)

    st = stencil.reshape(-1)
    field, a_mate, a_far, r_rows = call(
        load_kernel,
        "load",
        [smem(), vmem()],
        (f32(*shape), f32(HALO + 8, W), f32(HALO + 8, W), f32(8, W)),
    )(dev, rhs)
    g_far = swap(a_far, FAR)
    g_mate = swap(a_mate, MATE)
    ui, dots_ui, theta, stiff_v, mortar_v, dual_v, masks = call(
        inner_first_kernel,
        "inner_first",
        [anywhere()] + [smem()] * 2 + whole(2) + [anywhere()] * 2,
        (
            f32(*half),
            flat,
            f32(8, W),
            f32(PLANES, W, W),
            jax.ShapeDtypeStruct(mortar.shape, mortar.dtype),
            f32(PLANES, W),
            f32(104, W),
        ),
        [pltpu.VMEM((3, 12, W, W), F32), dma(3), flat_st],
        stage,
    )(st, partner, active, field, dual, stiff, mortar)
    own_faces = jnp.concatenate([a_mate[HALO : HALO + 4], g_mate[HALO : HALO + 4], g_far[HALO : HALO + 4]])
    own_faces, ui = lax.optimization_barrier((own_faces, ui))
    faces = swap(own_faces, CROSS)
    ue, dots_ue, b_mate, b_far = call(
        edge_first_kernel,
        "edge_first",
        [smem(), anywhere()] + whole(5),
        (f32(*half), flat, f32(HALO + 8, W), f32(HALO + 8, W)),
        [pltpu.VMEM((3, 18, W, W), F32), flat_st, dma()],
        stage,
    )(dev, st, field, g_mate, g_far, stiff_v, ui)
    faces, b_mate, b_far = lax.optimization_barrier((faces, b_mate, b_far))
    items, dots_c = call(
        contact0_kernel,
        "contact0",
        [smem()] + whole(6),
        (f32(16, W), f32(8, W)),
        [pltpu.VMEM((16, W), F32)],
    )(dev, masks, faces, g_far, r_rows, dual_v, mortar_v)
    u_rows = b_mate[HALO : HALO + 8]
    h_mate = swap(b_mate, MATE)
    mate_items = swap(items, MATE)
    h_far = swap(jnp.concatenate([b_far, items, mate_items[0:12]]), FAR)
    ki, dots_ki, stiff_rows, coefs = call(
        inner_second_kernel,
        "inner_second",
        [anywhere()] + whole(3),
        (f32(*half), flat, f32(8, W), f32(88, W)),
        [pltpu.VMEM((3, 12, W, W), F32), flat_st, dma()],
        stage,
    )(st, ui, ue, stiff_v)
    h_far, ki = lax.optimization_barrier((h_far, ki))
    h_next = swap(h_far[HALO + 8 : HALO + 20], MATE)
    pack = call(gather_kernel, "gather", whole(6), f32(72, W))(u_rows, h_mate, mate_items, h_far, h_next, items)
    cross = swap(pack, CROSS)
    ke, dots_ke, k_rows = call(
        edge_second_kernel,
        "edge_second",
        [smem(), anywhere()] + whole(6),
        (f32(*half), flat, f32(8, W)),
        [pltpu.VMEM((3, 18, W, W), F32), flat_st, dma()],
        stage,
    )(dev, st, ui, ue, h_mate, h_far, stiff_v, ki)
    send, rows = call(
        join_kernel,
        "join",
        [smem()] + whole(17),
        (f32(32, 8, W), f32(64, W)),
        [pltpu.VMEM((16, W), F32), pltpu.VMEM((16, W), F32)],
    )(
        dev, masks, coefs, mate_items, h_far, pack, cross, items, stiff_rows,
        u_rows, k_rows, dual_v, mortar_v, dots_ui, dots_ue, dots_c, dots_ki, dots_ke,
    )
    got = exchange(send, PLANE_GROUPS)
    relayed = call(relay_kernel, "relay", [smem(), vmem()], f32(8, 8, W))(dev, got)
    sums = exchange(relayed, COLUMN_GROUPS)
    return call(
        final_kernel,
        "final",
        whole(8),
        (f32(*shape), f32(*shape)),
        [pltpu.VMEM(shape, F32), pltpu.VMEM(shape, F32), pltpu.VMEM((W, W), F32), dma(2, 3, 4)],
        out_specs=(anywhere(), anywhere()),
    )(theta, field, ui, ue, ki, ke, rows, sums)


def solution(mesh):
    placed = (
        P(None, "slab", None, None),
        P("slab", None, None),
        P(),
        P("slab", None),
        P("slab", None, None, None),
        P("slab", None),
        P("slab"),
    )
    return jax.shard_map(
        local,
        mesh=mesh,
        in_specs=placed,
        out_specs=(P(None, "slab", None, None), P(None, "slab", None, None)),
        check_vma=False,
    )
```
